128 devices in a mesh: mem: 16 (over z, x), sub: 8 (over y, core).
Axes of the slice: x: 4, y: 4, z: 4, core: 2. Of those that a mesh axis runs over, the one named last changes fastest.
Arguments:
- ensemble: float32 [64, 3, 256, 2048], P('mem', None, 'sub'), may hold values from -6 to 6
- sea_depth: float32 [256, 2048], P('sub'), may hold values from 0.5 to 2
- cutoff: int32 [256, 2048], P('sub', 'mem'), may hold values from 16 to 64
- obs_index: int32 [4, 256], replicated, may hold values from 0 to 524287
- obs_value: float32 [4, 256], replicated, may hold values from -6 to 6
- obs_var: float32 [4, 256], replicated, may hold values from 0.5 to 2
Outputs:
- analysis: float32 [64, 3, 256, 2048], P(None, None, 'sub', 'mem')
The draws below stay inside these ranges and needn't reach their ends.
All inputs are finite; a program needn't handle non-finite values.
Results may differ from the reference program's by a relative error of at most 0.0001.
Values sent between devices are 32-bit elements; how exact they have to be, the bound alone decides.
A program may use at most 192 MiB of HBM per device.

```python
import math
import jax
import jax.numpy as jnp
from jax import lax

MEMBERS = 64
ROWS_DEV = 32
NX = 256
NY = 2048
STEPS = 4
NOBS = 256
BATCHES = 4


def set_ends(result, stream_key, least, largest):
    dims = result.shape
    index_at = [jax.random.randint(jax.random.fold_in(stream_key, axis), (), 0, dims[axis]) for axis in range(len(dims))]
    result = result.at[tuple(index_at)].set(least)
    longest = dims.index(max(dims))
    index_at[longest] = (index_at[longest] + 1) % dims[longest]
    return result.at[tuple(index_at)].set(largest)


def block_scale(key, shape, split, low, top_value):
    def one(dim, shards_of):
        heights = jax.random.uniform(jax.random.fold_in(jax.random.fold_in(key, 6), dim), (shards_of,), jnp.float32, low / len(split), top_value / len(split))
        return jnp.repeat(jnp.exp(heights), shape[dim] // shards_of).reshape((-1,) + (1,) * (len(shape) - dim - 1))

    loudness = one(*split[0])
    for cut in split[1:]:
        loudness = loudness * one(*cut)
    return loudness


def normal_values(rng, dims, spread, bound, shards=(), held_as=jnp.bfloat16):
    values = spread * jax.random.normal(rng, dims, jnp.float32)
    if shards:
        values = values * block_scale(rng, dims, shards, -0.22, 0.18)
    return jnp.clip(values, -bound, bound).astype(held_as)


def setup_inputs(seed: int = 0) -> dict:
    key_of = jax.random.split(jax.random.key(seed), 7)
    ensemble = normal_values(key_of[0], (MEMBERS, 3, NX, NY), 1.0, 6.0, ((0, 16), (2, 8)), jnp.float32)
    sea_depth = jnp.clip(jnp.exp(math.log(2.0) - 1.3862944 * jax.random.uniform(key_of[1], (NX, NY), jnp.float32) ** block_scale(key_of[1], (NX, NY), ((0, 8),), -0.2, 0.2)), 0.5, 2.0)
    cutoff = set_ends(jax.random.randint(key_of[2], (NX, NY), max(2, ROWS_DEV // 2), 2 * ROWS_DEV + 1), jax.random.fold_in(key_of[2], 1), max(2, ROWS_DEV // 2), 2 * ROWS_DEV).astype(jnp.int32)
    obs_index = set_ends(jax.random.randint(key_of[3], (BATCHES, NOBS), 0, NX * NY), jax.random.fold_in(key_of[3], 1), 0, (NX * NY) - 1).astype(jnp.int32)
    obs_value = normal_values(key_of[4], (BATCHES, NOBS), 1.0, 6.0, (), jnp.float32)
    obs_var = jnp.clip(jnp.exp(jax.random.uniform(key_of[5], (BATCHES, NOBS), jnp.float32, math.log(0.5), math.log(2.0))), 0.5, 2.0)
    return dict(ensemble=ensemble, sea_depth=sea_depth, cutoff=cutoff, obs_index=obs_index, obs_value=obs_value, obs_var=obs_var)


step_size = 0.3
coriolis = 0.2
highest = lax.Precision.HIGHEST

def centred(field, axis):
    return (jnp.roll(field, -1, axis) - jnp.roll(field, 1, axis)) * 0.5

def localize(obs_x, obs_y, cell_x, cell_y, radius_sq, size_x, size_y):
    gap_x = jnp.abs(cell_x[None, :] - obs_x[:, None])
    gap_x = jnp.minimum(gap_x, size_x - gap_x)
    gap_y = jnp.abs(cell_y[None, :] - obs_y[:, None])
    gap_y = jnp.minimum(gap_y, size_y - gap_y)
    dist_sq = (gap_x * gap_x + gap_y * gap_y).astype(jnp.float32)
    dist_ratio = dist_sq / radius_sq[None, :]
    return jnp.square(jnp.maximum(1.0 - dist_ratio, 0.0))

def analysis_weights(prior_obs, values, variance):
    member_count = prior_obs.shape[1]
    obs_mean = jnp.mean(prior_obs, 1)
    obs_anom = prior_obs - obs_mean[:, None]
    innov_cov = jnp.dot(obs_anom, obs_anom.T, precision=highest) / (member_count - 1) + jnp.diag(variance)
    factor = jnp.linalg.cholesky(innov_cov)
    right_side = jnp.concatenate([(values - obs_mean)[:, None], obs_anom], 1)
    solved = jax.scipy.linalg.cho_solve((factor, True), right_side)
    return (obs_anom, solved[:, :1] - 0.5 * solved[:, 1:])

def reference(ensemble, sea_depth, cutoff, obs_index, obs_value, obs_var):
    height = ensemble[:, 0]
    east_wind = ensemble[:, 1]
    north_wind = ensemble[:, 2]
    for step_id in range(STEPS):
        east_new = east_wind + step_size * (coriolis * north_wind - centred(height, 1))
        north_new = north_wind + step_size * (-coriolis * east_wind - centred(height, 2))
        divergence = centred(sea_depth * east_new, 1) + centred(sea_depth * north_new, 2)
        height = height - step_size * divergence
        east_wind = east_new
        north_wind = north_new
    point_state = jnp.stack([height, east_wind, north_wind], 1)
    grid_rows = jnp.transpose(point_state, (2, 0, 1, 3))
    col_ids = jnp.arange(NY, dtype=jnp.int32)
    row_ids = jnp.arange(NX, dtype=jnp.int32)
    radius_sq = jnp.square(cutoff.astype(jnp.float32))
    for batch_id in range(BATCHES):
        obs_cell = obs_index[batch_id]
        obs_x = (obs_cell // NY).astype(jnp.int32)
        obs_y = (obs_cell % NY).astype(jnp.int32)
        prior_obs = grid_rows[obs_x, :, 0, obs_y]
        obs_anom, weights_mix = analysis_weights(prior_obs, obs_value[batch_id], obs_var[batch_id])

        def update_row(items):
            grid_row, row_id, row_radius = items
            state_anom = grid_row - jnp.mean(grid_row, 0)
            cross_cov = jnp.einsum('om,mfy->ofy', obs_anom, state_anom, precision=highest) / (MEMBERS - 1)
            loc_weight = localize(obs_x, obs_y, jnp.zeros((NY,), jnp.int32) + row_id, col_ids, row_radius, NX, NY)
            loc_gain = cross_cov * loc_weight[:, None, :]
            return grid_row + jnp.einsum('om,ofy->mfy', weights_mix, loc_gain, precision=highest)
        grid_rows = lax.map(update_row, (grid_rows, row_ids, radius_sq))
    return jnp.transpose(grid_rows, (1, 2, 0, 3))
```

```python
import functools

import jax
import jax.numpy as jnp
from jax import lax
from jax.experimental import pallas as pl
from jax.experimental.pallas import tpu as pltpu
from jax.sharding import PartitionSpec as P

STEPS = 4
BATCHES = 4
DT = 0.3
CORIOLIS = 0.2
MESH = pl.DeviceIdType.MESH
HIGHEST = lax.Precision.HIGHEST
F32 = jnp.float32
BF16 = jnp.bfloat16
HALO = 8
CHUNK = 32
LANES = 128


def nt(a, b, precision=None):
    return lax.dot_general(
        a, b, (((1,), (1,)), ((), ())), precision=precision, preferred_element_type=F32
    )


def nn(a, b, precision=None):
    return lax.dot_general(
        a, b, (((1,), (0,)), ((), ())), precision=precision, preferred_element_type=F32
    )


def split2(x):
    hi = x.astype(BF16)
    return hi, (x - hi.astype(F32)).astype(BF16)


def iota(shape, dim):
    return lax.broadcasted_iota(jnp.int32, shape, dim)


def forecast_kernel(
    ens_ref, depth_ref, cut_ref, obs_ref,
    out_ref, prior_ref,
    ext, dep, gbuf, part, slots, mine,
    lsem, hs_sem, hr_sem, ds_sem, dr_sem, s1_sem, r1_sem, s2_sem, r2_sem,
):
    members, fields, rows, cols = ens_ref.shape
    tiles = cols // LANES
    me = lax.axis_index("mem")
    sub = lax.axis_index("sub")
    n_mem = lax.axis_size("mem")
    n_sub = lax.axis_size("sub")
    nobs = obs_ref.shape[1]

    barrier = pltpu.get_barrier_semaphore()
    for k in range(1, n_sub):
        pl.semaphore_signal(barrier, inc=1, device_id=(me, lax.rem(sub + k, n_sub)), device_id_type=MESH)
    for k in range(1, n_mem):
        pl.semaphore_signal(barrier, inc=1, device_id=(lax.rem(me + k, n_mem), sub), device_id_type=MESH)

    local = []
    cp = pltpu.make_async_copy(depth_ref, dep.at[pl.ds(HALO, rows)], lsem.at[members])
    cp.start()
    local.append(cp)
    for m in range(members):
        cp = pltpu.make_async_copy(ens_ref.at[m], ext.at[m, :, pl.ds(HALO, rows)], lsem.at[m])
        cp.start()
        local.append(cp)
    pl.semaphore_wait(barrier, n_sub - 1 + n_mem - 1)

    up = lax.rem(sub + n_sub - 1, n_sub)
    down = lax.rem(sub + 1, n_sub)
    halo = []
    for d, (peer, src, dst) in enumerate(((up, 0, HALO + rows), (down, rows - HALO, 0))):
        cp = pltpu.make_async_remote_copy(
            depth_ref.at[pl.ds(src, HALO)], dep.at[pl.ds(dst, HALO)],
            ds_sem.at[d], dr_sem.at[d], device_id=(me, peer), device_id_type=MESH)
        cp.start()
        halo.append(cp)
    for m in range(members):
        for d, (peer, src, dst) in enumerate(((up, 0, HALO + rows), (down, rows - HALO, 0))):
            cp = pltpu.make_async_remote_copy(
                ens_ref.at[m, :, pl.ds(src, HALO)], ext.at[m, :, pl.ds(dst, HALO)],
                hs_sem.at[d, m], hr_sem.at[d, m], device_id=(me, peer), device_id_type=MESH)
            cp.start()
            halo.append(cp)

    obs_x = obs_ref[0:1, :]
    obs_y = obs_ref[1:2, :]
    local_x = obs_x - sub * rows
    in_rows = (local_x >= 0) & (local_x < rows)
    combo = jnp.where(in_rows, (obs_y // LANES) * rows + local_x, -1)
    lane_of = obs_y % LANES

    in_block = in_rows & (obs_y // LANES == me)
    pick_row = jnp.where(in_block, local_x, -1)
    cut_t = jnp.transpose(cut_ref[...].astype(F32))
    row_hot = jnp.where(iota((rows, nobs), 0) == pick_row, 1.0, 0.0)
    cut_cols = nn(cut_t.astype(BF16), row_hot.astype(BF16))
    cut_obs = jnp.sum(jnp.where(iota((LANES, nobs), 0) == lane_of, cut_cols, 0.0), 0, keepdims=True)
    for q in range(nobs // LANES):
        mine[pl.ds(members * 8 + q, 1), :] = cut_obs[:, q * LANES:(q + 1) * LANES]

    halo[0].wait()
    halo[1].wait()
    for cp in local:
        cp.wait()
    for cp in halo[2:]:
        cp.wait()

    height = rows + 2 * HALO
    lane = iota((height, LANES), 1)

    def cols_of(t):
        return pl.ds(t * LANES, LANES)

    def member_body(m, _):
        def step_body(s, carry):
            def h_tile(t):
                return ext[m, 0, :, cols_of(t)]

            def g_tile(t):
                return gbuf[:, cols_of(t)]

            for t in range(tiles):
                h = h_tile(t)
                nxt = h_tile((t + 1) % tiles)
                prv = h_tile((t - 1) % tiles)
                east = jnp.where(lane < LANES - 1, pltpu.roll(h, LANES - 1, 1), pltpu.roll(nxt, LANES - 1, 1))
                west = jnp.where(lane > 0, pltpu.roll(h, 1, 1), pltpu.roll(prv, 1, 1))
                h_dx = (pltpu.roll(h, height - 1, 0) - pltpu.roll(h, 1, 0)) * 0.5
                h_dy = (east - west) * 0.5
                u = ext[m, 1, :, cols_of(t)]
                v = ext[m, 2, :, cols_of(t)]
                u1 = u + DT * (CORIOLIS * v - h_dx)
                v1 = v + DT * (-CORIOLIS * u - h_dy)
                ext[m, 1, :, cols_of(t)] = u1
                ext[m, 2, :, cols_of(t)] = v1
                gbuf[:, cols_of(t)] = dep[:, cols_of(t)] * v1
            for t in range(tiles):
                g = g_tile(t)
                nxt = g_tile((t + 1) % tiles)
                prv = g_tile((t - 1) % tiles)
                east = jnp.where(lane < LANES - 1, pltpu.roll(g, LANES - 1, 1), pltpu.roll(nxt, LANES - 1, 1))
                west = jnp.where(lane > 0, pltpu.roll(g, 1, 1), pltpu.roll(prv, 1, 1))
                f = dep[:, cols_of(t)] * ext[m, 1, :, cols_of(t)]
                f_dx = (pltpu.roll(f, height - 1, 0) - pltpu.roll(f, 1, 0)) * 0.5
                g_dy = (east - west) * 0.5
                ext[m, 0, :, cols_of(t)] = h_tile(t) - DT * (f_dx + g_dy)
            return carry

        lax.fori_loop(0, STEPS, step_body, 0)
        for f in range(fields):
            for t in range(tiles):
                out_ref[t, m, f] = ext[m, f, pl.ds(HALO, rows), cols_of(t)]
        block = 256
        turned = jnp.concatenate(
            [jnp.transpose(jnp.concatenate([ext[m, 0, pl.ds(HALO, rows), cols_of(t)] for t in range(4 * g, 4 * g + 4)], 0))
             for g in range(tiles // 4)], 1)
        hi = turned.astype(BF16)
        rest = turned - hi.astype(F32)
        mid = rest.astype(BF16)
        low = (rest - mid.astype(F32)).astype(BF16)
        parts = jnp.concatenate([hi, mid, low], 0)
        for q in range(nobs // block):
            span = slice(q * block, (q + 1) * block)
            hot = jnp.where(iota((tiles * rows, block), 0) == combo[:, span], 1.0, 0.0).astype(BF16)
            picked = nn(parts, hot)
            picked = picked[0:LANES] + picked[LANES:2 * LANES] + picked[2 * LANES:]
            got = jnp.sum(jnp.where(iota((LANES, block), 0) == lane_of[:, span], picked, 0.0), 0, keepdims=True)
            for s in range(block // LANES):
                mine[pl.ds(m * 8 + q * (block // LANES) + s, 1), :] = got[:, s * LANES:(s + 1) * LANES]
        return 0

    lax.fori_loop(0, members, member_body, 0)

    part[sub] = mine[...]
    first = []
    for k in range(1, n_sub):
        cp = pltpu.make_async_remote_copy(
            mine, part.at[sub], s1_sem.at[k], r1_sem.at[k],
            device_id=(me, lax.rem(sub + k, n_sub)), device_id_type=MESH)
        cp.start()
        first.append(cp)
    for cp in first:
        cp.wait()
    total = part[0]
    for k in range(1, n_sub):
        total = total + part[k]
    slots[...] = total
    prior_ref[me] = total
    second = []
    for k in range(1, n_mem):
        cp = pltpu.make_async_remote_copy(
            slots, prior_ref.at[me], s2_sem.at[k], r2_sem.at[k],
            device_id=(lax.rem(me + k, n_mem), sub), device_id_type=MESH)
        cp.start()
        second.append(cp)
    for cp in second:
        cp.wait()


def forecast(ensemble, sea_depth, cutoff, obs_xy):
    members, fields, rows, cols = ensemble.shape
    n_mem = lax.axis_size("mem")
    n_sub = lax.axis_size("sub")
    nobs = obs_xy.shape[1]
    tiles = cols // LANES
    width = members * 8 + nobs // LANES
    vmem = pl.BlockSpec(memory_space=pltpu.VMEM)
    hbm = pl.BlockSpec(memory_space=pl.ANY)
    dma = pltpu.SemaphoreType.DMA
    return pl.pallas_call(
        forecast_kernel,
        out_shape=(
            jax.ShapeDtypeStruct((tiles, members, fields, rows, LANES), F32),
            jax.ShapeDtypeStruct((n_mem, width, LANES), F32),
        ),
        in_specs=[hbm, hbm, vmem, vmem],
        out_specs=(vmem, vmem),
        scratch_shapes=[
            pltpu.VMEM((members, fields, rows + 2 * HALO, cols), F32),
            pltpu.VMEM((rows + 2 * HALO, cols), F32),
            pltpu.VMEM((rows + 2 * HALO, cols), F32),
            pltpu.VMEM((n_sub, width, LANES), F32),
            pltpu.VMEM((width, LANES), F32),
            pltpu.VMEM((width, LANES), F32),
            dma((members + 1,)), dma((2, members)), dma((2, members)), dma((2,)), dma((2,)),
            dma((n_sub,)), dma((n_sub,)), dma((n_mem,)), dma((n_mem,)),
        ],
        compiler_params=pltpu.CompilerParams(
            collective_id=0, has_side_effects=True, vmem_limit_bytes=56 << 20),
        name="forecast",
    )(ensemble, sea_depth, cutoff, obs_xy)


def weights_kernel(prior_ref, obs_ref, val_ref, var_ref, at_ref, wt_ref, flat, heights, cuts, *, size_x, size_y):
    n_mem, width, _ = prior_ref.shape
    batches, members, nobs = at_ref.shape
    per = members // n_mem
    groups = batches * nobs // LANES
    flat[...] = prior_ref[:, 0:per * 8, :].reshape(members * 8, LANES)
    cut = jnp.sum(prior_ref[:, per * 8:per * 8 + groups, :], 0)
    for q in range(groups):
        b, s = q * LANES // nobs, q * LANES % nobs
        heights[b, :, s:s + LANES] = flat[pl.ds(q, members, stride=8), :]
        cuts[b, :, s:s + LANES] = cut[q:q + 1, :]
    scale = 1.0 / (members - 1)

    def batch_body(b, _):
        h = heights[b]
        mean = jnp.mean(h, 0, keepdims=True)
        at = h - mean
        inv_var = 1.0 / var_ref[b]
        scaled = at * inv_var
        gram = nt(scaled, at, HIGHEST) * scale
        eye = jnp.where(iota((members, members), 0) == iota((members, members), 1), 1.0, 0.0)
        aug = jnp.concatenate([gram + eye, eye], 1)

        def eliminate(g, x):
            for j in range(8):
                col = jnp.broadcast_to(x[:, j:j + 1], x.shape)
                row = x[j:j + 1, :] / col[j:j + 1, :]
                fixed = x - col * row
                x = jnp.where(iota(x.shape, 0) == j, row, fixed)
            x = jnp.concatenate([x[8:], x[:8]], 0)
            return pltpu.roll(x, x.shape[1] - 8, 1)

        aug = lax.fori_loop(0, members // 8, eliminate, aug)
        inverse = aug[:, 0:members]
        big = nn(inverse, scaled, HIGHEST)
        gap = (val_ref[b] - mean) * inv_var
        lean = jnp.sum(at * gap, 1, keepdims=True)
        small = gap - scale * jnp.sum(big * lean, 0, keepdims=True)
        wt = small - 0.5 * big
        at_ref[b] = at * scale
        wt_ref[b] = wt

        xy = jnp.transpose(jnp.broadcast_to(obs_ref[b, 0:1, :].astype(F32), (8, nobs)))
        yy = jnp.transpose(jnp.broadcast_to(obs_ref[b, 1:2, :].astype(F32), (8, nobs)))
        from_x = xy[:, 0:1]
        from_y = yy[:, 0:1]
        anom = jnp.transpose(at * scale)

        def carry_body(c, _):
            hc = heights[c]
            dev = hc - jnp.mean(hc, 0, keepdims=True)
            cross = nn(anom, dev, HIGHEST)
            gx = jnp.abs(obs_ref[c, 0:1, :].astype(F32) - from_x)
            gx = jnp.minimum(gx, size_x - gx)
            gy = jnp.abs(obs_ref[c, 1:2, :].astype(F32) - from_y)
            gy = jnp.minimum(gy, size_y - gy)
            radius = cuts[c]
            near = jnp.maximum(1.0 - (gx * gx + gy * gy) / (radius * radius), 0.0)
            heights[c] = hc + nn(wt, cross * (near * near), HIGHEST)
            return 0

        lax.fori_loop(b + 1, batches, carry_body, 0)
        return 0

    lax.fori_loop(0, batches, batch_body, 0)


def weights(prior, obs, values, variance, members, size_x, size_y):
    batches, _, nobs = obs.shape
    vmem = pl.BlockSpec(memory_space=pltpu.VMEM)
    return pl.pallas_call(
        functools.partial(weights_kernel, size_x=float(size_x), size_y=float(size_y)),
        out_shape=(jax.ShapeDtypeStruct((batches, members, nobs), F32),) * 2,
        in_specs=[vmem] * 4,
        out_specs=(vmem, vmem),
        scratch_shapes=[
            pltpu.VMEM((members * 8, LANES), F32),
            pltpu.VMEM((batches, members, nobs), F32),
            pltpu.VMEM((batches, 1, nobs), F32),
        ],
        compiler_params=pltpu.CompilerParams(vmem_limit_bytes=16 << 20),
        cost_estimate=pl.CostEstimate(flops=200_000_000, bytes_accessed=2_000_000, transcendentals=0),
        name="weights",
    )(prior, obs, values, variance)


def update_kernel(state_ref, at_ref, wt_ref, obs_ref, cut_ref, out_ref,
                  lhs1, lhs2, far_x, sq_y, inv_r2, work, rhs1, rhs2, counts):
    members, fields, block, _ = state_ref.shape
    batches, _, nobs = at_ref.shape
    rows = cut_ref.shape[0]
    step = pl.program_id(0)
    size_x = rows * lax.axis_size("sub")
    size_y = LANES * lax.axis_size("mem")
    x0 = lax.axis_index("sub") * rows
    y0 = lax.axis_index("mem") * LANES

    @pl.when(step == 0)
    def _():
        cut = cut_ref[...].astype(F32)
        inv_r2[...] = 1.0 / (cut * cut)
        top = jnp.max(cut_ref[...])
        reach = top * top
        upper = jnp.where(iota((nobs, nobs), 0) < iota((nobs, nobs), 1), 1.0, 0.0).astype(BF16)

        def gap_to(pos, low, length, size):
            before = low - pos
            before = jnp.where(before < 0, before + size, before)
            after = pos - (low + length - 1)
            after = jnp.where(after < 0, after + size, after)
            inside = (pos >= low) & (pos < low + length)
            return jnp.where(inside, 0, jnp.minimum(before, after))

        def select(b, _):
            ox = obs_ref[b, 0:1, :]
            oy = obs_ref[b, 1:2, :]
            gx = gap_to(ox, x0, rows, size_x)
            gy = gap_to(oy, y0, LANES, size_y)
            keep = jnp.where(gx * gx + gy * gy < reach, 1.0, 0.0)
            rank = nn(jnp.broadcast_to(keep, (16, nobs)).astype(BF16), upper)[0:1]
            rank = jnp.where(keep > 0.5, rank, -1.0)
            total = jnp.sum(keep).astype(jnp.int32)
            chunks = (total + CHUNK - 1) // CHUNK
            counts[b] = chunks
            a_hi, a_lo = split2(at_ref[b])
            w_hi, w_lo = split2(wt_ref[b])
            a3 = jnp.concatenate([a_hi, a_hi, a_lo], 0)
            w2 = jnp.concatenate([w_hi, w_lo], 1)

            def pack(c, _):
                want = (iota((CHUNK, nobs), 0) + c * CHUNK).astype(F32)
                hot = jnp.where(rank == want, 1.0, 0.0)
                hot16 = hot.astype(BF16)
                lhs1[b, c] = nt(hot16, a3).astype(BF16)
                zero = jnp.zeros_like(hot16)
                turn = jnp.concatenate(
                    [jnp.concatenate([hot16, hot16, zero], 0), jnp.concatenate([zero, zero, hot16], 0)], 1)
                lhs2[b, c] = nt(w2, turn).astype(BF16)
                px = jnp.sum(hot * ox.astype(F32), 1, keepdims=True)
                py = jnp.sum(hot * oy.astype(F32), 1, keepdims=True)
                far_x[b, c] = jnp.broadcast_to(px, (CHUNK, LANES))
                gy = jnp.abs((iota((CHUNK, LANES), 1) + y0).astype(F32) - py)
                gy = jnp.minimum(gy, size_y - gy)
                sq_y[b, c] = gy * gy
                return 0

            lax.fori_loop(0, chunks, pack, 0)
            return 0

        lax.fori_loop(0, batches, select, 0)

    slabs = fields * block
    source = state_ref.reshape(members * slabs, LANES)
    target = out_ref.reshape(members * slabs, LANES)
    for s in range(slabs):
        work[:, s * LANES:(s + 1) * LANES] = source[pl.ds(s, members, stride=slabs), :]

    def batch_body(b, _):
        for s in range(slabs):
            span = slice(s * LANES, (s + 1) * LANES)
            x = work[:, span]
            hi, lo = split2(x - jnp.mean(x, 0, keepdims=True))
            rhs1[0:members, span] = hi
            rhs1[members:2 * members, span] = lo
            rhs1[2 * members:, span] = hi

        def chunk_body(c, _):
            left = lhs1[b, c]
            right = lhs2[b, c]
            px = far_x[b, c]
            dy = sq_y[b, c]
            for r in range(0, block, 2):
                near = []
                for k in (r, r + 1):
                    row = step * block + k
                    gx = jnp.abs(px - (x0 + row).astype(F32))
                    gx = jnp.minimum(gx, size_x - gx)
                    ratio = (gx * gx + dy) * inv_r2[pl.ds(row, 1), :]
                    part = jnp.maximum(1.0 - ratio, 0.0)
                    near.append(part * part)
                near = jnp.concatenate(near, 1)
                for f in range(fields):
                    s = f * block + r
                    span = slice(s * LANES, (s + 2) * LANES)
                    hi, lo = split2(nn(left, rhs1[:, span]) * near)
                    work[:, span] += nn(right, jnp.concatenate([hi, lo, hi], 0))
            return 0

        lax.fori_loop(0, counts[b], chunk_body, 0)
        return 0

    lax.fori_loop(0, batches, batch_body, 0)
    for s in range(slabs):
        target[pl.ds(s, members, stride=slabs), :] = work[:, s * LANES:(s + 1) * LANES]


def update(state, at, wt, obs, cutoff):
    members, fields, rows, _ = state.shape
    batches, _, nobs = at.shape
    block = 8
    chunks = nobs // CHUNK
    whole = pl.BlockSpec((members, fields, block, LANES), lambda i: (0, 0, i, 0))
    vmem = pl.BlockSpec(memory_space=pltpu.VMEM)
    width = fields * block * LANES
    return pl.pallas_call(
        update_kernel,
        out_shape=jax.ShapeDtypeStruct(state.shape, F32),
        grid=(rows // block,),
        in_specs=[whole, vmem, vmem, vmem, vmem],
        out_specs=whole,
        scratch_shapes=[
            pltpu.VMEM((batches, chunks, CHUNK, 3 * members), BF16),
            pltpu.VMEM((batches, chunks, members, 3 * CHUNK), BF16),
            pltpu.VMEM((batches, chunks, CHUNK, LANES), F32),
            pltpu.VMEM((batches, chunks, CHUNK, LANES), F32),
            pltpu.VMEM((rows, LANES), F32),
            pltpu.VMEM((members, width), F32),
            pltpu.VMEM((3 * members, width), BF16),
            pltpu.VMEM((3 * CHUNK, width), BF16),
            pltpu.SMEM((batches,), jnp.int32),
        ],
        compiler_params=pltpu.CompilerParams(vmem_limit_bytes=40 << 20),
        name="update",
    )(state, at, wt, obs, cutoff)


def local(ensemble, sea_depth, cutoff, obs_index, obs_value, obs_var):
    per, fields, rows, cols = ensemble.shape
    members = per * lax.axis_size("mem")
    size_x = rows * lax.axis_size("sub")
    obs_x = obs_index // cols
    obs_y = obs_index % cols
    obs = jnp.stack([obs_x, obs_y], 1)
    flat = jnp.stack([obs_x.reshape(-1), obs_y.reshape(-1)], 0)
    blocks, prior = forecast(ensemble, sea_depth, cutoff, flat)
    state = lax.all_to_all(
        blocks.reshape(cols // LANES, per * fields * rows, LANES), "mem", split_axis=0, concat_axis=0, tiled=True)
    at, wt = weights(prior, obs, obs_value[:, None, :], obs_var[:, None, :], members, size_x, cols)
    return update(state.reshape(members, fields, rows, LANES), at, wt, obs, cutoff)


def solution(mesh):
    return jax.shard_map(
        local,
        mesh=mesh,
        in_specs=(P("mem", None, "sub", None), P("sub", None), P("sub", "mem"), P(), P(), P()),
        out_specs=P(None, None, "sub", "mem"),
        check_vma=False,
    )
```

```python
import functools

import jax
import jax.numpy as jnp
from jax import lax
from jax.experimental import pallas as pl
from jax.experimental.pallas import tpu as pltpu
from jax.sharding import PartitionSpec as P

STEPS = 4
BATCHES = 4
DT = 0.3
CORIOLIS = 0.2
MESH = pl.DeviceIdType.MESH
HIGHEST = lax.Precision.HIGHEST
F32 = jnp.float32
BF16 = jnp.bfloat16
HALO = 8
CHUNK = 32
LANES = 128


def nt(a, b, precision=None):
    return lax.dot_general(
        a, b, (((1,), (1,)), ((), ())), precision=precision, preferred_element_type=F32
    )


def nn(a, b, precision=None):
    return lax.dot_general(
        a, b, (((1,), (0,)), ((), ())), precision=precision, preferred_element_type=F32
    )


def split2(x):
    hi = x.astype(BF16)
    return hi, (x - hi.astype(F32)).astype(BF16)


def iota(shape, dim):
    return lax.broadcasted_iota(jnp.int32, shape, dim)


SIDE = 4
ORDER = (
    (0, 1), (0, 3), (1, 0), (3, 0), (1, 1), (3, 3), (1, 3), (3, 1),
    (0, 2), (2, 0), (2, 1), (2, 3), (1, 2), (3, 2), (2, 2),
)
EARLY = 15


def forecast_kernel(
    ens_ref, depth_ref, cut_ref, obs_ref, batch_ref, val_ref, var_ref,
    out_ref, at_ref, wt_ref,
    ext, dep, hbuf, fbuf, gbuf, part, slots, mine, prior_ref, staged, flat, heights, cuts,
    lsem, hs_sem, hr_sem, ds_sem, dr_sem, s1_sem, r1_sem, s2_sem, r2_sem, bs_sem, br_sem, own_sem,
):
    members, fields, rows, cols = ens_ref.shape
    tiles = cols // LANES
    me = lax.axis_index("mem")
    sub = lax.axis_index("sub")
    n_mem = lax.axis_size("mem")
    n_sub = lax.axis_size("sub")
    nobs = obs_ref.shape[1]

    barrier = pltpu.get_barrier_semaphore()
    for k in range(1, n_sub):
        pl.semaphore_signal(barrier, inc=1, device_id=(me, lax.rem(sub + k, n_sub)), device_id_type=MESH)
    for k in range(1, n_mem):
        pl.semaphore_signal(barrier, inc=1, device_id=(lax.rem(me + k, n_mem), sub), device_id_type=MESH)

    local = []
    cp = pltpu.make_async_copy(depth_ref, dep.at[pl.ds(HALO, rows)], lsem.at[members])
    cp.start()
    local.append(cp)
    for m in range(members):
        cp = pltpu.make_async_copy(ens_ref.at[m], ext.at[m, :, pl.ds(HALO, rows)], lsem.at[m])
        cp.start()
        local.append(cp)
    pl.semaphore_wait(barrier, n_sub - 1 + n_mem - 1)

    up = lax.rem(sub + n_sub - 1, n_sub)
    down = lax.rem(sub + 1, n_sub)
    halo = []
    for d, (peer, src, dst) in enumerate(((up, 0, HALO + rows), (down, rows - HALO, 0))):
        cp = pltpu.make_async_remote_copy(
            depth_ref.at[pl.ds(src, HALO)], dep.at[pl.ds(dst, HALO)],
            ds_sem.at[d], dr_sem.at[d], device_id=(me, peer), device_id_type=MESH)
        cp.start()
        halo.append(cp)

    def halo_copies(m):
        return [
            pltpu.make_async_remote_copy(
                ens_ref.at[m, :, pl.ds(src, HALO)], ext.at[m, :, pl.ds(dst, HALO)],
                hs_sem.at[d, m], hr_sem.at[d, m], device_id=(me, peer), device_id_type=MESH)
            for d, (peer, src, dst) in enumerate(((up, 0, HALO + rows), (down, rows - HALO, 0)))
        ]

    for m in range(members):
        for cp in halo_copies(m):
            cp.start()

    obs_x = obs_ref[0:1, :]
    obs_y = obs_ref[1:2, :]
    local_x = obs_x - sub * rows
    in_rows = (local_x >= 0) & (local_x < rows)
    combo = jnp.where(in_rows, (obs_y // LANES) * rows + local_x, -1)
    lane_of = obs_y % LANES

    in_block = in_rows & (obs_y // LANES == me)
    pick_row = jnp.where(in_block, local_x, -1)
    cut_t = jnp.transpose(cut_ref[...].astype(F32))
    row_hot = jnp.where(iota((rows, nobs), 0) == pick_row, 1.0, 0.0)
    cut_cols = nn(cut_t.astype(BF16), row_hot.astype(BF16))
    cut_obs = jnp.sum(jnp.where(iota((LANES, nobs), 0) == lane_of, cut_cols, 0.0), 0, keepdims=True)
    for q in range(nobs // LANES):
        mine[pl.ds(members * 8 + q, 1), :] = cut_obs[:, q * LANES:(q + 1) * LANES]

    halo[0].wait()
    halo[1].wait()
    local[0].wait()

    height = rows + 2 * HALO
    lane = iota((height, LANES), 1)
    here, above, below = (pl.ds(HALO + k, height) for k in (0, 1, -1))
    pad = jnp.zeros((HALO, LANES), F32)
    for buf in (hbuf, fbuf):
        for t in range(tiles):
            buf[t, 0:HALO] = pad
            buf[t, HALO + height:] = pad

    def cols_of(t):
        return pl.ds(t * LANES, LANES)

    def spread(load):
        first_east = pltpu.roll(load(0), LANES - 1, 1)
        east = first_east
        west_before = pltpu.roll(load(tiles - 1), 1, 1)
        for t in range(tiles):
            east_next = first_east if t == tiles - 1 else pltpu.roll(load(t + 1), LANES - 1, 1)
            west = pltpu.roll(load(t), 1, 1)
            yield t, jnp.where(lane < LANES - 1, east, east_next) - jnp.where(lane > 0, west, west_before)
            east, west_before = east_next, west

    half = 0.5 * DT

    def block_copies(m, first, last):
        found = []
        for n, (dz, dx) in list(enumerate(ORDER))[first:last]:
            peer = lax.rem(me // SIDE + dz, SIDE) * SIDE + lax.rem(lax.rem(me, SIDE) + dx, SIDE)
            found.append(pltpu.make_async_remote_copy(
                staged.at[peer, m], out_ref.at[me, m], bs_sem.at[n, m], br_sem.at[n, m],
                device_id=(peer, sub), device_id_type=MESH))
        return found

    def own_copy(m):
        return pltpu.make_async_copy(staged.at[me, m], out_ref.at[me, m], own_sem.at[m])

    def member_body(m, _):
        pltpu.make_async_copy(ens_ref.at[m], ext.at[m, :, pl.ds(HALO, rows)], lsem.at[m]).wait()
        for cp in halo_copies(m):
            cp.wait()
        for t in range(tiles):
            hbuf[t, here] = ext[m, 0, :, cols_of(t)]

        def step_body(s, carry):
            for t, h_dy in spread(lambda t: hbuf[t, here]):
                u = ext[m, 1, :, cols_of(t)]
                v = ext[m, 2, :, cols_of(t)]
                u1 = u + ((DT * CORIOLIS) * v - half * (hbuf[t, above] - hbuf[t, below]))
                v1 = v - ((DT * CORIOLIS) * u + half * h_dy)
                d = dep[:, cols_of(t)]
                ext[m, 1, :, cols_of(t)] = u1
                ext[m, 2, :, cols_of(t)] = v1
                fbuf[t, here] = d * u1
                gbuf[t] = d * v1
            for t, g_dy in spread(lambda t: gbuf[t]):
                hbuf[t, here] = hbuf[t, here] - half * (fbuf[t, above] - fbuf[t, below] + g_dy)
            return carry

        lax.fori_loop(0, STEPS, step_body, 0)
        inner = pl.ds(2 * HALO, rows)
        for t in range(tiles):
            staged[t, m, 0] = hbuf[t, inner]
            for f in range(1, fields):
                staged[t, m, f] = ext[m, f, pl.ds(HALO, rows), cols_of(t)]
        own_copy(m).start()

        @pl.when(m == 0)
        def _():
            for cp in block_copies(m, 0, EARLY):
                cp.start()

        block = 256
        turned = jnp.concatenate(
            [jnp.transpose(jnp.concatenate([hbuf[t, inner] for t in range(4 * g, 4 * g + 4)], 0))
             for g in range(tiles // 4)], 1)
        hi = turned.astype(BF16)
        rest = turned - hi.astype(F32)
        mid = rest.astype(BF16)
        low = (rest - mid.astype(F32)).astype(BF16)
        parts = jnp.concatenate([hi, mid, low], 0)
        for q in range(nobs // block):
            span = slice(q * block, (q + 1) * block)
            hot = jnp.where(iota((tiles * rows, block), 0) == combo[:, span], 1.0, 0.0).astype(BF16)
            picked = nn(parts, hot)
            picked = picked[0:LANES] + picked[LANES:2 * LANES] + picked[2 * LANES:]
            got = jnp.sum(jnp.where(iota((LANES, block), 0) == lane_of[:, span], picked, 0.0), 0, keepdims=True)
            for s in range(block // LANES):
                mine[pl.ds(m * 8 + q * (block // LANES) + s, 1), :] = got[:, s * LANES:(s + 1) * LANES]
        return 0

    lax.fori_loop(0, members, member_body, 0)

    part[sub] = mine[...]
    first = []
    for k in range(1, n_sub):
        cp = pltpu.make_async_remote_copy(
            mine, part.at[sub], s1_sem.at[k], r1_sem.at[k],
            device_id=(me, lax.rem(sub + k, n_sub)), device_id_type=MESH)
        cp.start()
        first.append(cp)
    for cp in first:
        cp.wait()
    total = part[0]
    for k in range(1, n_sub):
        total = total + part[k]
    slots[...] = total
    prior_ref[me] = total
    second = []
    for k in range(1, n_mem):
        cp = pltpu.make_async_remote_copy(
            slots, prior_ref.at[me], s2_sem.at[k], r2_sem.at[k],
            device_id=(lax.rem(me + k, n_mem), sub), device_id_type=MESH)
        cp.start()
        second.append(cp)
    for cp in block_copies(0, EARLY, len(ORDER)):
        cp.start()

    def rest_body(m, _):
        for cp in block_copies(m, 0, len(ORDER)):
            cp.start()
        return 0

    lax.fori_loop(1, members, rest_body, 0)
    for cp in second:
        cp.wait()
    weights(prior_ref, batch_ref, val_ref, var_ref, at_ref, wt_ref, flat, heights, cuts,
            float(rows * n_sub), float(cols))

    def finish_body(m, _):
        for cp in block_copies(m, 0, len(ORDER)):
            cp.wait()
        own_copy(m).wait()
        return 0

    lax.fori_loop(0, members, finish_body, 0)


def nn3(a, b):
    a_hi, a_lo = split2(a)
    b_hi, b_lo = split2(b)
    return nn(a_hi, b_hi) + (nn(a_hi, b_lo) + nn(a_lo, b_hi))


def weights(prior_ref, obs_ref, val_ref, var_ref, at_ref, wt_ref, flat, heights, cuts, size_x, size_y):
    n_mem, width, _ = prior_ref.shape
    batches, members, nobs = at_ref.shape
    per = members // n_mem
    groups = batches * nobs // LANES
    flat[...] = prior_ref[:, 0:per * 8, :].reshape(members * 8, LANES)
    cut = jnp.sum(prior_ref[:, per * 8:per * 8 + groups, :], 0)
    cut = 1.0 / (cut * cut)
    for q in range(groups):
        b, s = q * LANES // nobs, q * LANES % nobs
        heights[b, :, s:s + LANES] = flat[pl.ds(q, members, stride=8), :]
        cuts[b, :, s:s + LANES] = cut[q:q + 1, :]
    scale = 1.0 / (members - 1)

    def batch_body(b, _):
        h = heights[b]
        mean = jnp.mean(h, 0, keepdims=True)
        at = h - mean
        inv_var = 1.0 / var_ref[b]
        scaled = at * inv_var
        gram = nt(scaled, at, HIGHEST) * scale
        eye = jnp.where(iota((members, members), 0) == iota((members, members), 1), 1.0, 0.0)
        aug = jnp.concatenate([gram + eye, eye], 1)

        def eliminate(g, x):
            for j in range(0, 8, 2):
                col0 = jnp.broadcast_to(x[:, j:j + 1], x.shape)
                col1 = jnp.broadcast_to(x[:, j + 1:j + 2], x.shape)
                a, b01, c = col0[j:j + 1], col1[j:j + 1], col1[j + 1:j + 2]
                inv = 1.0 / (a * c - b01 * b01)
                row0 = (c * x[j:j + 1] - b01 * x[j + 1:j + 2]) * inv
                row1 = (a * x[j + 1:j + 2] - b01 * x[j:j + 1]) * inv
                fixed = x - col0 * row0 - col1 * row1
                x = jnp.where(iota(x.shape, 0) == j, row0, jnp.where(iota(x.shape, 0) == j + 1, row1, fixed))
            x = jnp.concatenate([x[8:], x[:8]], 0)
            return pltpu.roll(x, x.shape[1] - 8, 1)

        aug = lax.fori_loop(0, members // 8, eliminate, aug)
        inverse = aug[:, 0:members]
        big = nn(inverse, scaled, HIGHEST)
        gap = (val_ref[b] - mean) * inv_var
        lean = jnp.sum(at * gap, 1, keepdims=True)
        small = gap - scale * jnp.sum(big * lean, 0, keepdims=True)
        wt = small - 0.5 * big
        at_ref[b] = at * scale
        wt_ref[b] = wt

        xy = jnp.concatenate([jnp.broadcast_to(obs_ref[b, k:k + 1, :].astype(F32), (4, nobs)) for k in range(2)], 0)
        xy = jnp.transpose(xy)
        from_x = xy[:, 0:1]
        from_y = xy[:, 4:5]
        anom_hi, anom_lo = split2(jnp.transpose(at * scale))
        wt_hi, wt_lo = split2(wt)

        def carry_body(c, _):
            hc = heights[c]
            dev_hi, dev_lo = split2(hc - jnp.mean(hc, 0, keepdims=True))
            cross = nn(anom_hi, dev_hi) + (nn(anom_hi, dev_lo) + nn(anom_lo, dev_hi))
            gx = jnp.abs(obs_ref[c, 0:1, :].astype(F32) - from_x)
            gx = jnp.minimum(gx, size_x - gx)
            gy = jnp.abs(obs_ref[c, 1:2, :].astype(F32) - from_y)
            gy = jnp.minimum(gy, size_y - gy)
            near = jnp.maximum(1.0 - (gx * gx + gy * gy) * cuts[c], 0.0)
            gain_hi, gain_lo = split2(cross * (near * near))
            heights[c] = hc + (nn(wt_hi, gain_hi) + (nn(wt_hi, gain_lo) + nn(wt_lo, gain_hi)))
            return 0

        lax.fori_loop(b + 1, batches, carry_body, 0)
        return 0

    lax.fori_loop(0, batches, batch_body, 0)


def forecast(ensemble, sea_depth, cutoff, obs_xy, obs, values, variance):
    per, fields, rows, cols = ensemble.shape
    n_mem = lax.axis_size("mem")
    n_sub = lax.axis_size("sub")
    members = per * n_mem
    batches, _, nobs = obs.shape
    total = batches * nobs
    tiles = cols // LANES
    width = per * 8 + total // LANES
    vmem = pl.BlockSpec(memory_space=pltpu.VMEM)
    hbm = pl.BlockSpec(memory_space=pl.ANY)
    dma = pltpu.SemaphoreType.DMA
    vm = pltpu.VMEM
    return pl.pallas_call(
        forecast_kernel,
        out_shape=(
            jax.ShapeDtypeStruct((n_mem, per, fields, rows, LANES), F32),
            jax.ShapeDtypeStruct((batches, members, nobs), F32),
            jax.ShapeDtypeStruct((batches, members, nobs), F32),
        ),
        in_specs=[hbm, hbm] + [vmem] * 5,
        out_specs=(hbm, vmem, vmem),
        scratch_shapes=[
            vm((per, fields, rows + 2 * HALO, cols), F32),
            vm((rows + 2 * HALO, cols), F32),
            vm((tiles, rows + 4 * HALO, LANES), F32),
            vm((tiles, rows + 4 * HALO, LANES), F32),
            vm((tiles, rows + 2 * HALO, LANES), F32),
            vm((n_sub, width, LANES), F32),
            vm((width, LANES), F32),
            vm((width, LANES), F32),
            vm((n_mem, width, LANES), F32),
            vm((tiles, per, fields, rows, LANES), F32),
            vm((members * 8, LANES), F32),
            vm((batches, members, nobs), F32),
            vm((batches, 1, nobs), F32),
            dma((per + 1,)), dma((2, per)), dma((2, per)), dma((2,)), dma((2,)),
            dma((n_sub,)), dma((n_sub,)), dma((n_mem,)), dma((n_mem,)),
            dma((n_mem, per)), dma((n_mem, per)), dma((per,)),
        ],
        compiler_params=pltpu.CompilerParams(
            collective_id=0, has_side_effects=True, vmem_limit_bytes=56 << 20),
        name="forecast",
    )(ensemble, sea_depth, cutoff, obs_xy, obs, values, variance)


def update_kernel(state_ref, at_ref, wt_ref, obs_ref, cut_ref, out_ref,
                  lhs1, lhs2, far_x, sq_y, inv_r2, work, rhs1, begin, stage, counts, in_sems, sems):
    members, fields, rows, _ = state_ref.shape
    batches, _, nobs = at_ref.shape
    block = work.shape[1] // (fields * LANES)
    size_x = rows * lax.axis_size("sub")
    size_y = LANES * lax.axis_size("mem")
    x0 = lax.axis_index("sub") * rows
    y0 = lax.axis_index("mem") * LANES

    for step in range(rows // block):
        pltpu.make_async_copy(
            state_ref.at[:, :, pl.ds(step * block, block)], begin.at[step], in_sems.at[step]).start()
    cut = cut_ref[...].astype(F32)
    inv_r2[...] = 1.0 / (cut * cut)
    top = jnp.max(cut_ref[...])
    reach = top * top
    upper = jnp.where(iota((nobs, nobs), 0) < iota((nobs, nobs), 1), 1.0, 0.0).astype(BF16)

    def gap_to(pos, low, length, size):
        before = low - pos
        before = jnp.where(before < 0, before + size, before)
        after = pos - (low + length - 1)
        after = jnp.where(after < 0, after + size, after)
        inside = (pos >= low) & (pos < low + length)
        return jnp.where(inside, 0, jnp.minimum(before, after))

    def select(b, _):
        ox = obs_ref[b, 0:1, :]
        oy = obs_ref[b, 1:2, :]
        gx = gap_to(ox, x0, rows, size_x)
        gy = gap_to(oy, y0, LANES, size_y)
        keep = jnp.where(gx * gx + gy * gy < reach, 1.0, 0.0)
        rank = nn(jnp.broadcast_to(keep, (16, nobs)).astype(BF16), upper)[0:1]
        rank = jnp.where(keep > 0.5, rank, -1.0)
        total = jnp.sum(keep).astype(jnp.int32)
        chunks = (total + CHUNK - 1) // CHUNK
        counts[b] = chunks
        a = at_ref[b]
        a_hi, a_lo = split2(a - jnp.mean(a, 0, keepdims=True))
        w_hi, w_lo = split2(wt_ref[b])
        a3 = jnp.concatenate([a_hi, a_hi, a_lo], 0)
        w2 = jnp.concatenate([w_hi, w_lo], 1)

        def pack(c, _):
            want = (iota((CHUNK, nobs), 0) + c * CHUNK).astype(F32)
            hot = jnp.where(rank == want, 1.0, 0.0)
            hot16 = hot.astype(BF16)
            lhs1[b, c] = nt(hot16, a3).astype(BF16)
            zero = jnp.zeros_like(hot16)
            turn = jnp.concatenate(
                [jnp.concatenate([hot16, hot16, zero], 0), jnp.concatenate([zero, zero, hot16], 0)], 1)
            lhs2[b, c] = nt(w2, turn).astype(BF16)
            px = jnp.sum(hot * ox.astype(F32), 1, keepdims=True)
            py = jnp.sum(hot * oy.astype(F32), 1, keepdims=True)
            far_x[b, c] = jnp.broadcast_to(px, (CHUNK, LANES))
            gy = jnp.abs((iota((CHUNK, LANES), 1) + y0).astype(F32) - py)
            gy = jnp.minimum(gy, size_y - gy)
            sq_y[b, c] = gy * gy
            return 0

        lax.fori_loop(0, chunks, pack, 0)
        return 0

    lax.fori_loop(0, batches, select, 0)

    slabs = fields * block
    steps = rows // block

    def place(s):
        return pl.ds(s % fields * block + s // fields, members, stride=slabs)

    def part(step):
        return pl.ds(pl.multiple_of(step * block, block), block)

    def in_copy(step):
        return pltpu.make_async_copy(state_ref.at[:, :, part(step)], begin.at[step], in_sems.at[step])

    def out_copy(step):
        return pltpu.make_async_copy(stage.at[step], out_ref.at[:, :, part(step)], sems.at[step])

    def step_body(step, _):
        in_copy(step).wait()
        source = begin.at[step].reshape(members * slabs, LANES)
        target = stage.at[step].reshape(members * slabs, LANES)
        for s in range(slabs):
            work[:, s * LANES:(s + 1) * LANES] = source[place(s), :]

        def batch_body(b, _):
            for s in range(slabs):
                span = slice(s * LANES, (s + 1) * LANES)
                hi, lo = split2(work[:, span])
                rhs1[0:members, span] = hi
                rhs1[members:2 * members, span] = lo
                rhs1[2 * members:, span] = hi

            def chunk_body(c, _):
                left = lhs1[b, c]
                right = lhs2[b, c]
                px = far_x[b, c]
                dy = sq_y[b, c]
                for r in range(0, block, 2):
                    near = []
                    for k in (r, r + 1):
                        row = step * block + k
                        gx = jnp.abs(px - (x0 + row).astype(F32))
                        gx = jnp.minimum(gx, size_x - gx)
                        ratio = (gx * gx + dy) * inv_r2[pl.ds(row, 1), :]
                        part = jnp.maximum(1.0 - ratio, 0.0)
                        near += [part * part] * fields
                    near = jnp.concatenate(near, 1)
                    span = slice(r * fields * LANES, (r + 2) * fields * LANES)
                    hi, lo = split2(nn(left, rhs1[:, span]) * near)
                    work[:, span] += nn(right, jnp.concatenate([hi, lo, hi], 0))
                return 0

            lax.fori_loop(0, counts[b], chunk_body, 0)
            return 0

        lax.fori_loop(0, batches, batch_body, 0)
        for s in range(slabs):
            target[place(s), :] = work[:, s * LANES:(s + 1) * LANES]
        out_copy(step).start()
        return 0

    lax.fori_loop(0, steps, step_body, 0)
    for step in range(steps):
        out_copy(step).wait()


def update(state, at, wt, obs, cutoff):
    members, fields, rows, _ = state.shape
    batches, _, nobs = at.shape
    block = 8
    chunks = nobs // CHUNK
    vmem = pl.BlockSpec(memory_space=pltpu.VMEM)
    width = fields * block * LANES
    return pl.pallas_call(
        update_kernel,
        out_shape=jax.ShapeDtypeStruct(state.shape, F32),
        in_specs=[pl.BlockSpec(memory_space=pl.ANY)] + [vmem] * 4,
        out_specs=pl.BlockSpec(memory_space=pl.ANY),
        scratch_shapes=[
            pltpu.VMEM((batches, chunks, CHUNK, 3 * members), BF16),
            pltpu.VMEM((batches, chunks, members, 3 * CHUNK), BF16),
            pltpu.VMEM((batches, chunks, CHUNK, LANES), F32),
            pltpu.VMEM((batches, chunks, CHUNK, LANES), F32),
            pltpu.VMEM((rows, LANES), F32),
            pltpu.VMEM((members, width), F32),
            pltpu.VMEM((3 * members, width), BF16),
            pltpu.VMEM((rows // block, members, fields, block, LANES), F32),
            pltpu.VMEM((rows // block, members, fields, block, LANES), F32),
            pltpu.SMEM((batches,), jnp.int32),
            pltpu.SemaphoreType.DMA((rows // block,)),
            pltpu.SemaphoreType.DMA((rows // block,)),
        ],
        compiler_params=pltpu.CompilerParams(vmem_limit_bytes=40 << 20),
        name="update",
    )(state, at, wt, obs, cutoff)


def local(ensemble, sea_depth, cutoff, obs_index, obs_value, obs_var):
    per, fields, rows, cols = ensemble.shape
    members = per * lax.axis_size("mem")
    obs_x = obs_index // cols
    obs_y = obs_index % cols
    obs = jnp.stack([obs_x, obs_y], 1)
    flat = jnp.stack([obs_x.reshape(-1), obs_y.reshape(-1)], 0)
    state, at, wt = forecast(ensemble, sea_depth, cutoff, flat, obs, obs_value[:, None, :], obs_var[:, None, :])
    return update(state.reshape(members, fields, rows, LANES), at, wt, obs, cutoff)


def solution(mesh):
    return jax.shard_map(
        local,
        mesh=mesh,
        in_specs=(P("mem", None, "sub", None), P("sub", None), P("sub", "mem"), P(), P(), P()),
        out_specs=P(None, None, "sub", "mem"),
        check_vma=False,
    )
```

```python
import functools

import jax
import jax.numpy as jnp
from jax import lax
from jax.experimental import pallas as pl
from jax.experimental.pallas import tpu as pltpu
from jax.sharding import PartitionSpec as P

STEPS = 4
BATCHES = 4
DT = 0.3
CORIOLIS = 0.2
MESH = pl.DeviceIdType.MESH
HIGHEST = lax.Precision.HIGHEST
F32 = jnp.float32
BF16 = jnp.bfloat16
HALO = 8
CHUNK = 32
GROUP = 8
LANES = 128


def nt(a, b, precision=None):
    return lax.dot_general(
        a, b, (((1,), (1,)), ((), ())), precision=precision, preferred_element_type=F32
    )


def nn(a, b, precision=None):
    return lax.dot_general(
        a, b, (((1,), (0,)), ((), ())), precision=precision, preferred_element_type=F32
    )


def split2(x):
    hi = x.astype(BF16)
    return hi, (x - hi.astype(F32)).astype(BF16)


def quot(x, size):
    return x >> (size.bit_length() - 1)


def rest(x, size):
    return x & (size - 1)


def iota(shape, dim):
    return lax.broadcasted_iota(jnp.int32, shape, dim)


SIDE = 4
ORDER = (
    (0, 1), (0, 3), (1, 0), (3, 0), (1, 1), (3, 3), (1, 3), (3, 1),
    (0, 2), (2, 0), (2, 1), (2, 3), (1, 2), (3, 2), (2, 2),
)
EARLY = 2


def forecast_kernel(
    ens_ref, depth_ref, cut_ref, obs_ref, val_ref, var_ref,
    out_ref, at_ref, wt_ref,
    ext, dep, hbuf, fbuf, gbuf, part, slots, mine, prior_ref, staged, flat, heights, cuts,
    lsem, hs_sem, hr_sem, ds_sem, dr_sem, s1_sem, r1_sem, s2_sem, r2_sem, bs_sem, br_sem, own_sem,
):
    members, fields, rows, cols = ens_ref.shape
    tiles = cols // LANES
    me = lax.axis_index("mem")
    sub = lax.axis_index("sub")
    n_mem = lax.axis_size("mem")
    n_sub = lax.axis_size("sub")
    nobs = obs_ref.shape[0] * obs_ref.shape[1]

    barrier = pltpu.get_barrier_semaphore()
    for k in range(1, n_sub):
        pl.semaphore_signal(barrier, inc=1, device_id=(me, lax.rem(sub + k, n_sub)), device_id_type=MESH)
    for k in range(1, n_mem):
        pl.semaphore_signal(barrier, inc=1, device_id=(lax.rem(me + k, n_mem), sub), device_id_type=MESH)

    local = []
    cp = pltpu.make_async_copy(depth_ref, dep.at[pl.ds(HALO, rows)], lsem.at[members])
    cp.start()
    local.append(cp)
    for m in range(members):
        cp = pltpu.make_async_copy(ens_ref.at[m], ext.at[m, :, pl.ds(HALO, rows)], lsem.at[m])
        cp.start()
        local.append(cp)
    pl.semaphore_wait(barrier, n_sub - 1 + n_mem - 1)

    up = lax.rem(sub + n_sub - 1, n_sub)
    down = lax.rem(sub + 1, n_sub)
    halo = []
    for d, (peer, src, dst) in enumerate(((up, 0, HALO + rows), (down, rows - HALO, 0))):
        cp = pltpu.make_async_remote_copy(
            depth_ref.at[pl.ds(src, HALO)], dep.at[pl.ds(dst, HALO)],
            ds_sem.at[d], dr_sem.at[d], device_id=(me, peer), device_id_type=MESH)
        cp.start()
        halo.append(cp)

    def halo_copies(m):
        return [
            pltpu.make_async_remote_copy(
                ens_ref.at[m, :, pl.ds(src, HALO)], ext.at[m, :, pl.ds(dst, HALO)],
                hs_sem.at[d, m], hr_sem.at[d, m], device_id=(me, peer), device_id_type=MESH)
            for d, (peer, src, dst) in enumerate(((up, 0, HALO + rows), (down, rows - HALO, 0)))
        ]

    for m in range(members):
        for cp in halo_copies(m):
            cp.start()

    index = jnp.concatenate([obs_ref[b:b + 1, :] for b in range(obs_ref.shape[0])], 1)
    obs_x = quot(index, cols)
    obs_y = rest(index, cols)
    local_x = obs_x - sub * rows
    in_rows = (local_x >= 0) & (local_x < rows)
    combo = jnp.where(in_rows, quot(obs_y, LANES) * rows + local_x, -1)
    lane_of = rest(obs_y, LANES)

    in_block = in_rows & (quot(obs_y, LANES) == me)
    pick_row = jnp.where(in_block, local_x, -1)
    cut_t = jnp.transpose(cut_ref[...].astype(F32))
    row_hot = jnp.where(iota((rows, nobs), 0) == pick_row, 1.0, 0.0)
    cut_cols = nn(cut_t.astype(BF16), row_hot.astype(BF16))
    cut_obs = jnp.sum(jnp.where(iota((LANES, nobs), 0) == lane_of, cut_cols, 0.0), 0, keepdims=True)
    for q in range(nobs // LANES):
        mine[pl.ds(members * 8 + q, 1), :] = cut_obs[:, q * LANES:(q + 1) * LANES]

    halo[0].wait()
    halo[1].wait()
    local[0].wait()

    height = rows + 2 * HALO
    lane = iota((height, LANES), 1)
    here, above, below = (pl.ds(HALO + k, height) for k in (0, 1, -1))
    pad = jnp.zeros((HALO, LANES), F32)
    for buf in (hbuf, fbuf):
        for t in range(tiles):
            buf[t, 0:HALO] = pad
            buf[t, HALO + height:] = pad

    def cols_of(t):
        return pl.ds(t * LANES, LANES)

    def spread(load):
        first_east = pltpu.roll(load(0), LANES - 1, 1)
        east = first_east
        west_before = pltpu.roll(load(tiles - 1), 1, 1)
        for t in range(tiles):
            east_next = first_east if t == tiles - 1 else pltpu.roll(load(t + 1), LANES - 1, 1)
            west = pltpu.roll(load(t), 1, 1)
            yield t, jnp.where(lane < LANES - 1, east, east_next) - jnp.where(lane > 0, west, west_before)
            east, west_before = east_next, west

    half = 0.5 * DT

    def block_copies(m, first, last):
        found = []
        for n, (dz, dx) in list(enumerate(ORDER))[first:last]:
            peer = lax.rem(me // SIDE + dz, SIDE) * SIDE + lax.rem(lax.rem(me, SIDE) + dx, SIDE)
            found.append(pltpu.make_async_remote_copy(
                staged.at[peer, m], out_ref.at[me, m], bs_sem.at[n, m], br_sem.at[n, m],
                device_id=(peer, sub), device_id_type=MESH))
        return found

    def own_copy(m):
        return pltpu.make_async_copy(staged.at[me, m], out_ref.at[me, m], own_sem.at[m])

    def member_body(m, _):
        pltpu.make_async_copy(ens_ref.at[m], ext.at[m, :, pl.ds(HALO, rows)], lsem.at[m]).wait()
        for cp in halo_copies(m):
            cp.wait()
        for t in range(tiles):
            hbuf[t, here] = ext[m, 0, :, cols_of(t)]

        def step_body(s, carry):
            for t, h_dy in spread(lambda t: hbuf[t, here]):
                u = ext[m, 1, :, cols_of(t)]
                v = ext[m, 2, :, cols_of(t)]
                u1 = u + ((DT * CORIOLIS) * v - half * (hbuf[t, above] - hbuf[t, below]))
                v1 = v - ((DT * CORIOLIS) * u + half * h_dy)
                d = dep[:, cols_of(t)]
                ext[m, 1, :, cols_of(t)] = u1
                ext[m, 2, :, cols_of(t)] = v1
                fbuf[t, here] = d * u1
                gbuf[t] = d * v1
            for t, g_dy in spread(lambda t: gbuf[t]):
                hbuf[t, here] = hbuf[t, here] - half * (fbuf[t, above] - fbuf[t, below] + g_dy)
            return carry

        lax.fori_loop(0, STEPS, step_body, 0)
        inner = pl.ds(2 * HALO, rows)
        for t in range(tiles):
            staged[t, m, 0] = hbuf[t, inner]
            for f in range(1, fields):
                staged[t, m, f] = ext[m, f, pl.ds(HALO, rows), cols_of(t)]
        own_copy(m).start()

        @pl.when(m < EARLY)
        def _():
            for cp in block_copies(m, 0, len(ORDER)):
                cp.start()

        block = 256
        turned = jnp.concatenate(
            [jnp.transpose(jnp.concatenate([hbuf[t, inner] for t in range(4 * g, 4 * g + 4)], 0))
             for g in range(tiles // 4)], 1)
        hi = turned.astype(BF16)
        rest = turned - hi.astype(F32)
        mid = rest.astype(BF16)
        low = (rest - mid.astype(F32)).astype(BF16)
        parts = jnp.concatenate([hi, mid, low], 0)
        for q in range(nobs // block):
            span = slice(q * block, (q + 1) * block)
            hot = jnp.where(iota((tiles * rows, block), 0) == combo[:, span], 1.0, 0.0).astype(BF16)
            picked = nn(parts, hot)
            picked = picked[0:LANES] + picked[LANES:2 * LANES] + picked[2 * LANES:]
            got = jnp.sum(jnp.where(iota((LANES, block), 0) == lane_of[:, span], picked, 0.0), 0, keepdims=True)
            for s in range(block // LANES):
                mine[pl.ds(m * 8 + q * (block // LANES) + s, 1), :] = got[:, s * LANES:(s + 1) * LANES]
        return 0

    lax.fori_loop(0, members, member_body, 0)

    part[sub] = mine[...]
    first = []
    for k in range(1, n_sub):
        cp = pltpu.make_async_remote_copy(
            mine, part.at[sub], s1_sem.at[k], r1_sem.at[k],
            device_id=(me, lax.rem(sub + k, n_sub)), device_id_type=MESH)
        cp.start()
        first.append(cp)
    for cp in first:
        cp.wait()
    total = part[0]
    for k in range(1, n_sub):
        total = total + part[k]
    slots[...] = total
    prior_ref[me] = total
    second = []
    for k in range(1, n_mem):
        cp = pltpu.make_async_remote_copy(
            slots, prior_ref.at[me], s2_sem.at[k], r2_sem.at[k],
            device_id=(lax.rem(me + k, n_mem), sub), device_id_type=MESH)
        cp.start()
        second.append(cp)
    def rest_body(m, _):
        for cp in block_copies(m, 0, len(ORDER)):
            cp.start()
        return 0

    lax.fori_loop(EARLY, members, rest_body, 0)
    for cp in second:
        cp.wait()
    weights(prior_ref, obs_ref, val_ref, var_ref, at_ref, wt_ref, flat, heights, cuts,
            rows * n_sub, cols)

    def finish_body(m, _):
        for cp in block_copies(m, 0, len(ORDER)):
            cp.wait()
        own_copy(m).wait()
        return 0

    lax.fori_loop(0, members, finish_body, 0)


def nn3(a, b):
    a_hi, a_lo = split2(a)
    b_hi, b_lo = split2(b)
    return nn(a_hi, b_hi) + (nn(a_hi, b_lo) + nn(a_lo, b_hi))


def weights(prior_ref, obs_ref, val_ref, var_ref, at_ref, wt_ref, flat, heights, cuts, size_x, size_y):
    n_mem, width, _ = prior_ref.shape
    batches, members, nobs = at_ref.shape
    per = members // n_mem
    groups = batches * nobs // LANES
    flat[...] = prior_ref[:, 0:per * 8, :].reshape(members * 8, LANES)
    cut = jnp.sum(prior_ref[:, per * 8:per * 8 + groups, :], 0)
    cut = 1.0 / (cut * cut)
    for q in range(groups):
        b, s = q * LANES // nobs, q * LANES % nobs
        heights[b, :, s:s + LANES] = flat[pl.ds(q, members, stride=8), :]
        cuts[b, :, s:s + LANES] = cut[q:q + 1, :]
    scale = 1.0 / (members - 1)

    def batch_body(b, _):
        h = heights[b]
        mean = jnp.mean(h, 0, keepdims=True)
        at = h - mean
        inv_var = 1.0 / var_ref[pl.ds(b, 1), :]
        scaled = at * inv_var
        gram = nt(scaled, at, HIGHEST) * scale
        eye = jnp.where(iota((members, members), 0) == iota((members, members), 1), 1.0, 0.0)
        x = jnp.concatenate([eye, gram + eye], 1)
        line = iota(x.shape, 0)
        for k in range(0, members, 8):
            ahead = [jnp.broadcast_to(x[:, members + k + l:members + k + l + 1], x.shape) for l in range(8)]
            for j in range(0, 8, 2):
                p, q = k + j, k + j + 1
                col0, col1 = ahead[0], ahead[1]
                a, b01, c = col0[p:p + 1], col1[p:p + 1], col1[q:q + 1]
                inv = 1.0 / (a * c - b01 * b01)
                a, b01, c = a * inv, b01 * inv, c * inv

                def sweep(y):
                    row0 = c * y[p:p + 1] - b01 * y[q:q + 1]
                    row1 = a * y[q:q + 1] - b01 * y[p:p + 1]
                    left = y - col0 * row0 - col1 * row1
                    return jnp.where(line == p, row0, jnp.where(line == q, row1, left))

                ahead = [sweep(y) for y in ahead[2:]]
                x = sweep(x)
        inverse = x[:, 0:members]
        big = nn3(inverse, scaled)
        gap = (val_ref[pl.ds(b, 1), :] - mean) * inv_var
        lean = jnp.sum(at * gap, 1, keepdims=True)
        small = gap - scale * jnp.sum(big * lean, 0, keepdims=True)
        wt = small - 0.5 * big
        at_ref[b] = at * scale
        wt_ref[b] = wt

        here = obs_ref[pl.ds(b, 1), :]
        xy = jnp.concatenate(
            [jnp.broadcast_to(k.astype(F32), (4, nobs)) for k in (quot(here, size_y), rest(here, size_y))], 0)
        xy = jnp.transpose(xy)
        from_x = xy[:, 0:1]
        from_y = xy[:, 4:5]
        anom_hi, anom_lo = split2(jnp.transpose(at * scale))
        wt_hi, wt_lo = split2(wt)

        def carry_body(c, _):
            hc = heights[c]
            dev_hi, dev_lo = split2(hc - jnp.mean(hc, 0, keepdims=True))
            cross = nn(anom_hi, dev_hi) + (nn(anom_hi, dev_lo) + nn(anom_lo, dev_hi))
            there = obs_ref[pl.ds(c, 1), :]
            gx = jnp.abs(quot(there, size_y).astype(F32) - from_x)
            gx = jnp.minimum(gx, size_x - gx)
            gy = jnp.abs(rest(there, size_y).astype(F32) - from_y)
            gy = jnp.minimum(gy, size_y - gy)
            near = jnp.maximum(1.0 - (gx * gx + gy * gy) * cuts[c], 0.0)
            gain_hi, gain_lo = split2(cross * (near * near))
            heights[c] = hc + (nn(wt_hi, gain_hi) + (nn(wt_hi, gain_lo) + nn(wt_lo, gain_hi)))
            return 0

        lax.fori_loop(b + 1, batches, carry_body, 0)
        return 0

    lax.fori_loop(0, batches, batch_body, 0)


def forecast(ensemble, sea_depth, cutoff, obs, values, variance):
    per, fields, rows, cols = ensemble.shape
    n_mem = lax.axis_size("mem")
    n_sub = lax.axis_size("sub")
    members = per * n_mem
    batches, nobs = obs.shape
    total = batches * nobs
    tiles = cols // LANES
    width = per * 8 + total // LANES
    vmem = pl.BlockSpec(memory_space=pltpu.VMEM)
    hbm = pl.BlockSpec(memory_space=pl.ANY)
    dma = pltpu.SemaphoreType.DMA
    vm = pltpu.VMEM
    return pl.pallas_call(
        forecast_kernel,
        out_shape=(
            jax.ShapeDtypeStruct((n_mem, per, fields, rows, LANES), F32),
            jax.ShapeDtypeStruct((batches, members, nobs), F32),
            jax.ShapeDtypeStruct((batches, members, nobs), F32),
        ),
        in_specs=[hbm, hbm] + [vmem] * 4,
        out_specs=(hbm, vmem, vmem),
        scratch_shapes=[
            vm((per, fields, rows + 2 * HALO, cols), F32),
            vm((rows + 2 * HALO, cols), F32),
            vm((tiles, rows + 4 * HALO, LANES), F32),
            vm((tiles, rows + 4 * HALO, LANES), F32),
            vm((tiles, rows + 2 * HALO, LANES), F32),
            vm((n_sub, width, LANES), F32),
            vm((width, LANES), F32),
            vm((width, LANES), F32),
            vm((n_mem, width, LANES), F32),
            vm((tiles, per, fields, rows, LANES), F32),
            vm((members * 8, LANES), F32),
            vm((batches, members, nobs), F32),
            vm((batches, 1, nobs), F32),
            dma((per + 1,)), dma((2, per)), dma((2, per)), dma((2,)), dma((2,)),
            dma((n_sub,)), dma((n_sub,)), dma((n_mem,)), dma((n_mem,)),
            dma((n_mem, per)), dma((n_mem, per)), dma((per,)),
        ],
        compiler_params=pltpu.CompilerParams(
            collective_id=0, has_side_effects=True, vmem_limit_bytes=56 << 20),
        name="forecast",
    )(ensemble, sea_depth, cutoff, obs, values, variance)


def update_kernel(state_ref, at_hbm, wt_hbm, obs_ref, cut_ref, out_ref,
                  at_ref, wt_ref, lhs1, lhs2, far_x, sq_y, inv_r2, work, begin, stage, counts, in_sems, sems, w_sems):
    members, fields, rows, _ = state_ref.shape
    batches, _, nobs = at_ref.shape
    block = work.shape[2] // (fields * LANES)
    size_x = rows * lax.axis_size("sub")
    size_y = LANES * lax.axis_size("mem")
    x0 = lax.axis_index("sub") * rows
    y0 = lax.axis_index("mem") * LANES

    early = [pltpu.make_async_copy(at_hbm, at_ref, w_sems.at[0]), pltpu.make_async_copy(wt_hbm, wt_ref, w_sems.at[1])]
    for cp in early:
        cp.start()
    for step in range(rows // block):
        pltpu.make_async_copy(
            state_ref.at[:, :, pl.ds(step * block, block)], begin.at[step], in_sems.at[step]).start()
    cut = cut_ref[...].astype(F32)
    inv_r2[...] = 1.0 / (cut * cut)
    top = jnp.max(cut_ref[...])
    reach = top * top
    upper = jnp.where(iota((nobs, nobs), 0) < iota((nobs, nobs), 1), 1.0, 0.0).astype(BF16)

    def gap_to(pos, low, length, size):
        before = low - pos
        before = jnp.where(before < 0, before + size, before)
        after = pos - (low + length - 1)
        after = jnp.where(after < 0, after + size, after)
        inside = (pos >= low) & (pos < low + length)
        return jnp.where(inside, 0, jnp.minimum(before, after))

    def select(b, _):
        ox = quot(obs_ref[pl.ds(b, 1), :], size_y)
        oy = rest(obs_ref[pl.ds(b, 1), :], size_y)
        gx = gap_to(ox, x0, rows, size_x)
        gy = gap_to(oy, y0, LANES, size_y)
        keep = jnp.where(gx * gx + gy * gy < reach, 1.0, 0.0)
        rank = nn(jnp.broadcast_to(keep, (16, nobs)).astype(BF16), upper)[0:1]
        rank = jnp.where(keep > 0.5, rank, -1.0)
        total = jnp.sum(keep).astype(jnp.int32)
        chunks = (total + CHUNK - 1) // CHUNK
        counts[b] = chunks
        a = at_ref[b]
        a_hi, a_lo = split2(a - jnp.mean(a, 0, keepdims=True))
        w_hi, w_lo = split2(wt_ref[b])
        a3 = jnp.concatenate([a_hi, a_hi, a_lo], 0)
        w2 = jnp.concatenate([w_hi, w_lo], 1)

        def pack(c, _):
            want = (iota((CHUNK, nobs), 0) + c * CHUNK).astype(F32)
            hot = jnp.where(rank == want, 1.0, 0.0)
            hot16 = hot.astype(BF16)
            lhs1[b, c] = nt(hot16, a3).astype(BF16)
            zero = jnp.zeros_like(hot16)
            turn = jnp.concatenate(
                [jnp.concatenate([hot16, hot16, zero], 0), jnp.concatenate([zero, zero, hot16], 0)], 1)
            lhs2[b, c] = nt(w2, turn).astype(BF16)
            px = jnp.sum(hot * ox.astype(F32), 1, keepdims=True)
            py = jnp.sum(hot * oy.astype(F32), 1, keepdims=True)
            far_x[b, c] = jnp.broadcast_to(px, (CHUNK, LANES))
            gy = jnp.abs((iota((CHUNK, LANES), 1) + y0).astype(F32) - py)
            gy = jnp.minimum(gy, size_y - gy)
            sq_y[b, c] = gy * gy
            return 0

        lax.fori_loop(0, chunks, pack, 0)
        return 0

    for cp in early:
        cp.wait()
    lax.fori_loop(0, batches, select, 0)

    slabs = fields * block
    steps = rows // block

    def place(s):
        return pl.ds(s % fields * block + s // fields, members, stride=slabs)

    def part(step):
        return pl.ds(pl.multiple_of(step * block, block), block)

    def in_copy(step):
        return pltpu.make_async_copy(state_ref.at[:, :, part(step)], begin.at[step], in_sems.at[step])

    def out_copy(step):
        return pltpu.make_async_copy(stage.at[step], out_ref.at[:, :, part(step)], sems.at[step])

    def step_body(step, _):
        in_copy(step).wait()
        source = begin.at[step].reshape(members * slabs, LANES)
        target = stage.at[step].reshape(members * slabs, LANES)
        for s in range(slabs):
            work[0, :, s * LANES:(s + 1) * LANES] = source[place(s), :]

        def batch_body(b, now):
            chunks = counts[b]

            def chunk_body(c, _):
                left = lhs1[b, c]
                right = lhs2[b, c]
                px = far_x[b, c]
                dy = sq_y[b, c]
                base = jnp.where(c == 0, now, 1 - now)
                for r in range(0, block, GROUP):
                    near = []
                    for k in range(r, r + GROUP):
                        row = step * block + k
                        gx = jnp.abs(px - (x0 + row).astype(F32))
                        gx = jnp.minimum(gx, size_x - gx)
                        ratio = (gx * gx + dy) * inv_r2[pl.ds(row, 1), :]
                        part = jnp.maximum(1.0 - ratio, 0.0)
                        near += [part * part] * fields
                    near = jnp.concatenate(near, 1)
                    span = slice(r * fields * LANES, (r + GROUP) * fields * LANES)
                    hi, lo = split2(work[now, :, span])
                    hi, lo = split2(nn(left, jnp.concatenate([hi, lo, hi], 0)) * near)
                    work[1 - now, :, span] = work[base, :, span] + nn(right, jnp.concatenate([hi, lo, hi], 0))
                return 0

            lax.fori_loop(0, chunks, chunk_body, 0)
            return jnp.where(chunks > 0, 1 - now, now)

        last = lax.fori_loop(0, batches, batch_body, 0)
        for s in range(slabs):
            target[place(s), :] = work[last, :, s * LANES:(s + 1) * LANES]
        out_copy(step).start()
        return 0

    lax.fori_loop(0, steps, step_body, 0)
    for step in range(steps):
        out_copy(step).wait()


def update(state, at, wt, obs, cutoff):
    members, fields, rows, _ = state.shape
    batches, _, nobs = at.shape
    block = 8
    chunks = nobs // CHUNK
    vmem = pl.BlockSpec(memory_space=pltpu.VMEM)
    width = fields * block * LANES
    return pl.pallas_call(
        update_kernel,
        out_shape=jax.ShapeDtypeStruct(state.shape, F32),
        in_specs=[pl.BlockSpec(memory_space=pl.ANY)] * 3 + [vmem] * 2,
        out_specs=pl.BlockSpec(memory_space=pl.ANY),
        scratch_shapes=[
            pltpu.VMEM(at.shape, F32),
            pltpu.VMEM(wt.shape, F32),
            pltpu.VMEM((batches, chunks, CHUNK, 3 * members), BF16),
            pltpu.VMEM((batches, chunks, members, 3 * CHUNK), BF16),
            pltpu.VMEM((batches, chunks, CHUNK, LANES), F32),
            pltpu.VMEM((batches, chunks, CHUNK, LANES), F32),
            pltpu.VMEM((rows, LANES), F32),
            pltpu.VMEM((2, members, width), F32),
            pltpu.VMEM((rows // block, members, fields, block, LANES), F32),
            pltpu.VMEM((rows // block, members, fields, block, LANES), F32),
            pltpu.SMEM((batches,), jnp.int32),
            pltpu.SemaphoreType.DMA((rows // block,)),
            pltpu.SemaphoreType.DMA((rows // block,)),
            pltpu.SemaphoreType.DMA((2,)),
        ],
        compiler_params=pltpu.CompilerParams(vmem_limit_bytes=63 << 20),
        name="update",
    )(state, at, wt, obs, cutoff)


def local(ensemble, sea_depth, cutoff, obs_index, obs_value, obs_var):
    per, fields, rows, cols = ensemble.shape
    members = per * lax.axis_size("mem")
    state, at, wt = forecast(ensemble, sea_depth, cutoff, obs_index, obs_value, obs_var)
    return update(state.reshape(members, fields, rows, LANES), at, wt, obs_index, cutoff)


def solution(mesh):
    return jax.shard_map(
        local,
        mesh=mesh,
        in_specs=(P("mem", None, "sub", None), P("sub", None), P("sub", "mem"), P(), P(), P()),
        out_specs=P(None, None, "sub", "mem"),
        check_vma=False,
    )
```

```python
import functools

import jax
import jax.numpy as jnp
from jax import lax
from jax.experimental import pallas as pl
from jax.experimental.pallas import tpu as pltpu
from jax.sharding import PartitionSpec as P

STEPS = 4
BATCHES = 4
DT = 0.3
CORIOLIS = 0.2
MESH = pl.DeviceIdType.MESH
HIGHEST = lax.Precision.HIGHEST
F32 = jnp.float32
BF16 = jnp.bfloat16
HALO = 8
CHUNK = 32
GROUP = 8
LANES = 128


def nt(a, b, precision=None):
    return lax.dot_general(
        a, b, (((1,), (1,)), ((), ())), precision=precision, preferred_element_type=F32
    )


def nn(a, b, precision=None):
    return lax.dot_general(
        a, b, (((1,), (0,)), ((), ())), precision=precision, preferred_element_type=F32
    )


def split2(x):
    hi = x.astype(BF16)
    return hi, (x - hi.astype(F32)).astype(BF16)


def quot(x, size):
    return x >> (size.bit_length() - 1)


def rest(x, size):
    return x & (size - 1)


def iota(shape, dim):
    return lax.broadcasted_iota(jnp.int32, shape, dim)


SIDE = 4
ORDER = (
    (0, 1), (0, 3), (1, 0), (3, 0), (1, 1), (3, 3), (1, 3), (3, 1),
    (0, 2), (2, 0), (2, 1), (2, 3), (1, 2), (3, 2), (2, 2),
)
EARLY = 2
SOME = 5


def forecast_kernel(
    ens_ref, depth_ref, cut_ref, obs_ref, val_ref, var_ref,
    out_ref, at_ref, wt_ref,
    ext, dep, hbuf, fbuf, gbuf, part, slots, mine, prior_ref, staged, flat, heights, cuts,
    lsem, hs_sem, hr_sem, ds_sem, dr_sem, s1_sem, r1_sem, s2_sem, r2_sem, bs_sem, br_sem, own_sem,
):
    members, fields, rows, cols = ens_ref.shape
    tiles = cols // LANES
    me = lax.axis_index("mem")
    sub = lax.axis_index("sub")
    n_mem = lax.axis_size("mem")
    n_sub = lax.axis_size("sub")
    nobs = obs_ref.shape[0] * obs_ref.shape[1]

    barrier = pltpu.get_barrier_semaphore()
    for k in range(1, n_sub):
        pl.semaphore_signal(barrier, inc=1, device_id=(me, lax.rem(sub + k, n_sub)), device_id_type=MESH)
    for k in range(1, n_mem):
        pl.semaphore_signal(barrier, inc=1, device_id=(lax.rem(me + k, n_mem), sub), device_id_type=MESH)

    local = []
    cp = pltpu.make_async_copy(depth_ref, dep.at[pl.ds(HALO, rows)], lsem.at[members])
    cp.start()
    local.append(cp)
    for m in range(members):
        cp = pltpu.make_async_copy(ens_ref.at[m], ext.at[m, :, pl.ds(HALO, rows)], lsem.at[m])
        cp.start()
        local.append(cp)
    pl.semaphore_wait(barrier, n_sub - 1 + n_mem - 1)

    up = lax.rem(sub + n_sub - 1, n_sub)
    down = lax.rem(sub + 1, n_sub)
    halo = []
    for d, (peer, src, dst) in enumerate(((up, 0, HALO + rows), (down, rows - HALO, 0))):
        cp = pltpu.make_async_remote_copy(
            depth_ref.at[pl.ds(src, HALO)], dep.at[pl.ds(dst, HALO)],
            ds_sem.at[d], dr_sem.at[d], device_id=(me, peer), device_id_type=MESH)
        cp.start()
        halo.append(cp)

    def halo_copies(m):
        return [
            pltpu.make_async_remote_copy(
                ens_ref.at[m, :, pl.ds(src, HALO)], ext.at[m, :, pl.ds(dst, HALO)],
                hs_sem.at[d, m], hr_sem.at[d, m], device_id=(me, peer), device_id_type=MESH)
            for d, (peer, src, dst) in enumerate(((up, 0, HALO + rows), (down, rows - HALO, 0)))
        ]

    for m in range(members):
        for cp in halo_copies(m):
            cp.start()

    index = jnp.concatenate([obs_ref[b:b + 1, :] for b in range(obs_ref.shape[0])], 1)
    obs_x = quot(index, cols)
    obs_y = rest(index, cols)
    local_x = obs_x - sub * rows
    in_rows = (local_x >= 0) & (local_x < rows)
    combo = jnp.where(in_rows, quot(obs_y, LANES) * rows + local_x, -1)
    lane_of = rest(obs_y, LANES)

    in_block = in_rows & (quot(obs_y, LANES) == me)
    pick_row = jnp.where(in_block, local_x, -1)
    cut_t = jnp.transpose(cut_ref[...].astype(F32))
    row_hot = jnp.where(iota((rows, nobs), 0) == pick_row, 1.0, 0.0)
    cut_cols = nn(cut_t.astype(BF16), row_hot.astype(BF16))
    cut_obs = jnp.sum(jnp.where(iota((LANES, nobs), 0) == lane_of, cut_cols, 0.0), 0, keepdims=True)
    for q in range(nobs // LANES):
        mine[0, q:q + 1, :] = cut_obs[:, q * LANES:(q + 1) * LANES]

    def send_part(s):
        part[sub, s] = mine[s]
        for k in range(1, n_sub):
            pltpu.make_async_remote_copy(
                mine.at[s], part.at[sub, s], s1_sem.at[s], r1_sem.at[s],
                device_id=(me, lax.rem(sub + k, n_sub)), device_id_type=MESH).start()

    def send_total(s):
        all_parts = part.at[pl.ds(0, n_sub - 1), s]
        pltpu.make_async_copy(all_parts, all_parts, r1_sem.at[s]).wait()
        total = part[0, s]
        for k in range(1, n_sub):
            total = total + part[k, s]
        slots[s] = total
        prior_ref[me, s] = total
        for k in range(1, n_mem):
            pltpu.make_async_remote_copy(
                slots.at[s], prior_ref.at[me, s], s2_sem.at[s], r2_sem.at[s],
                device_id=(lax.rem(me + k, n_mem), sub), device_id_type=MESH).start()

    send_part(0)

    halo[0].wait()
    halo[1].wait()
    local[0].wait()

    height = rows + 2 * HALO
    lane = iota((height, LANES), 1)
    here, above, below = (pl.ds(HALO + k, height) for k in (0, 1, -1))
    pad = jnp.zeros((HALO, LANES), F32)
    for buf in (hbuf, fbuf):
        for t in range(tiles):
            buf[t, 0:HALO] = pad
            buf[t, HALO + height:] = pad

    def cols_of(t):
        return pl.ds(t * LANES, LANES)

    def spread(load, lane):
        first_east = pltpu.roll(load(0), LANES - 1, 1)
        east = first_east
        west_before = pltpu.roll(load(tiles - 1), 1, 1)
        for t in range(tiles):
            east_next = first_east if t == tiles - 1 else pltpu.roll(load(t + 1), LANES - 1, 1)
            west = pltpu.roll(load(t), 1, 1)
            yield t, jnp.where(lane < LANES - 1, east, east_next) - jnp.where(lane > 0, west, west_before)
            east, west_before = east_next, west

    half = 0.5 * DT

    def block_copies(m, first, last):
        found = []
        for n, (dz, dx) in list(enumerate(ORDER))[first:last]:
            peer = lax.rem(me // SIDE + dz, SIDE) * SIDE + lax.rem(lax.rem(me, SIDE) + dx, SIDE)
            found.append(pltpu.make_async_remote_copy(
                staged.at[peer, m], out_ref.at[me, m], bs_sem.at[m], br_sem.at[m],
                device_id=(peer, sub), device_id_type=MESH))
        return found

    def own_copy(m):
        return pltpu.make_async_copy(staged.at[me, m], out_ref.at[me, m], own_sem.at[m])

    def member_body(m, _):
        pltpu.make_async_copy(ens_ref.at[m], ext.at[m, :, pl.ds(HALO, rows)], lsem.at[m]).wait()
        for cp in halo_copies(m):
            cp.wait()
        for t in range(tiles):
            hbuf[t, here] = ext[m, 0, :, cols_of(t)]

        def step_body(s, carry):
            for t, h_dy in spread(lambda t: hbuf[t, here], lane):
                u = ext[m, 1, :, cols_of(t)]
                v = ext[m, 2, :, cols_of(t)]
                u1 = u + ((DT * CORIOLIS) * v - half * (hbuf[t, above] - hbuf[t, below]))
                v1 = v - ((DT * CORIOLIS) * u + half * h_dy)
                d = dep[:, cols_of(t)]
                ext[m, 1, :, cols_of(t)] = u1
                ext[m, 2, :, cols_of(t)] = v1
                fbuf[t, here] = d * u1
                gbuf[t] = d * v1
            for t, g_dy in spread(lambda t: gbuf[t], lane):
                hbuf[t, here] = hbuf[t, here] - half * (fbuf[t, above] - fbuf[t, below] + g_dy)
            return carry

        lax.fori_loop(0, STEPS - 1, step_body, 0)
        inner = pl.ds(2 * HALO, rows)
        north, south = pl.ds(2 * HALO + 1, rows), pl.ds(2 * HALO - 1, rows)
        own = pl.ds(HALO, rows)
        for t, h_dy in spread(lambda t: hbuf[t, inner], lane[:rows]):
            u = ext[m, 1, :, cols_of(t)]
            v = ext[m, 2, :, cols_of(t)]
            u1 = u + ((DT * CORIOLIS) * v - half * (hbuf[t, above] - hbuf[t, below]))
            v1 = v[HALO:HALO + rows] - ((DT * CORIOLIS) * u[HALO:HALO + rows] + half * h_dy)
            d = dep[:, cols_of(t)]
            staged[t, m, 1] = u1[HALO:HALO + rows]
            staged[t, m, 2] = v1
            fbuf[t, here] = d * u1
            gbuf[t, own] = d[HALO:HALO + rows] * v1
        for t, g_dy in spread(lambda t: gbuf[t, own], lane[:rows]):
            staged[t, m, 0] = hbuf[t, inner] - half * (fbuf[t, north] - fbuf[t, south] + g_dy)
        own_copy(m).start()

        @pl.when(m < EARLY)
        def _():
            for cp in block_copies(m, 0, len(ORDER)):
                cp.start()

        @pl.when(m == EARLY)
        def _():
            for cp in block_copies(m, 0, SOME):
                cp.start()

        send_total(m)
        block = 256
        turned = jnp.concatenate(
            [jnp.transpose(jnp.concatenate([staged[t, m, 0] for t in range(4 * g, 4 * g + 4)], 0))
             for g in range(tiles // 4)], 1)
        parts = jnp.concatenate(split2(turned), 0)
        for q in range(nobs // block):
            span = slice(q * block, (q + 1) * block)
            hot = jnp.where(iota((tiles * rows, block), 0) == combo[:, span], 1.0, 0.0).astype(BF16)
            picked = nn(parts, hot)
            picked = picked[0:LANES] + picked[LANES:]
            got = jnp.sum(jnp.where(iota((LANES, block), 0) == lane_of[:, span], picked, 0.0), 0, keepdims=True)
            for s in range(block // LANES):
                mine[m + 1, pl.ds(q * (block // LANES) + s, 1), :] = got[:, s * LANES:(s + 1) * LANES]
        send_part(m + 1)
        return 0

    lax.fori_loop(0, members, member_body, 0)

    send_total(members)

    for cp in block_copies(EARLY, SOME, len(ORDER)):
        cp.start()

    def rest_body(m, _):
        for cp in block_copies(m, 0, len(ORDER)):
            cp.start()
        return 0

    lax.fori_loop(EARLY + 1, members, rest_body, 0)
    def totals_body(s, _):
        for sent, sems, count in ((part, s1_sem, n_sub), (prior_ref, s2_sem, n_mem), (prior_ref, r2_sem, n_mem)):
            peers = sent.at[pl.ds(0, count - 1), s]
            pltpu.make_async_copy(peers, peers, sems.at[s]).wait()
        return 0

    lax.fori_loop(0, members + 1, totals_body, 0)
    weights(prior_ref, obs_ref, val_ref, var_ref, at_ref, wt_ref, flat, heights, cuts,
            rows * n_sub, cols)

    def finish_body(m, _):
        peers = out_ref.at[pl.ds(0, n_mem - 1), m]
        for sems in (bs_sem, br_sem):
            pltpu.make_async_copy(peers, peers, sems.at[m]).wait()
        own_copy(m).wait()
        return 0

    lax.fori_loop(0, members, finish_body, 0)


def nn3(a, b):
    a_hi, a_lo = split2(a)
    b_hi, b_lo = split2(b)
    return nn(a_hi, b_hi) + (nn(a_hi, b_lo) + nn(a_lo, b_hi))


def weights(prior_ref, obs_ref, val_ref, var_ref, at_ref, wt_ref, flat, heights, cuts, size_x, size_y):
    n_mem, width, _, _ = prior_ref.shape
    batches, members, nobs = at_ref.shape
    groups = batches * nobs // LANES
    flat[...] = prior_ref[:, 1:].reshape(members * 8, LANES)
    cut = jnp.sum(prior_ref[:, 0], 0)
    cut = 1.0 / (cut * cut)
    for q in range(groups):
        b, s = q * LANES // nobs, q * LANES % nobs
        heights[b, :, s:s + LANES] = flat[pl.ds(q, members, stride=8), :]
        cuts[b, :, s:s + LANES] = cut[q:q + 1, :]
    scale = 1.0 / (members - 1)

    def batch_body(b, _):
        h = heights[b]
        mean = jnp.mean(h, 0, keepdims=True)
        at = h - mean
        inv_var = 1.0 / var_ref[pl.ds(b, 1), :]
        scaled = at * inv_var
        gram = nt(scaled, at, HIGHEST) * scale
        eye = jnp.where(iota((members, members), 0) == iota((members, members), 1), 1.0, 0.0)
        x = jnp.concatenate([eye, gram + eye], 1)
        line = iota(x.shape, 0)
        for k in range(0, members, 8):
            ahead = [jnp.broadcast_to(x[:, members + k + l:members + k + l + 1], x.shape) for l in range(8)]
            for j in range(0, 8, 2):
                p, q = k + j, k + j + 1
                col0, col1 = ahead[0], ahead[1]
                a, b01, c = col0[p:p + 1], col1[p:p + 1], col1[q:q + 1]
                inv = 1.0 / (a * c - b01 * b01)
                a, b01, c = a * inv, b01 * inv, c * inv

                def sweep(y):
                    row0 = c * y[p:p + 1] - b01 * y[q:q + 1]
                    row1 = a * y[q:q + 1] - b01 * y[p:p + 1]
                    left = y - col0 * row0 - col1 * row1
                    return jnp.where(line == p, row0, jnp.where(line == q, row1, left))

                ahead = [sweep(y) for y in ahead[2:]]
                x = sweep(x)
        inverse = x[:, 0:members]
        big = nn3(inverse, scaled)
        gap = (val_ref[pl.ds(b, 1), :] - mean) * inv_var
        lean = jnp.sum(at * gap, 1, keepdims=True)
        small = gap - scale * jnp.sum(big * lean, 0, keepdims=True)
        wt = small - 0.5 * big
        at_ref[b] = at * scale
        wt_ref[b] = wt

        here = obs_ref[pl.ds(b, 1), :]
        xy = jnp.concatenate(
            [jnp.broadcast_to(k.astype(F32), (4, nobs)) for k in (quot(here, size_y), rest(here, size_y))], 0)
        xy = jnp.transpose(xy)
        from_x = xy[:, 0:1]
        from_y = xy[:, 4:5]
        anom_hi, anom_lo = split2(jnp.transpose(at * scale))
        wt_hi, wt_lo = split2(wt)

        def carry_body(c, _):
            hc = heights[c]
            dev_hi, dev_lo = split2(hc - jnp.mean(hc, 0, keepdims=True))
            cross = nn(anom_hi, dev_hi) + (nn(anom_hi, dev_lo) + nn(anom_lo, dev_hi))
            there = obs_ref[pl.ds(c, 1), :]
            gx = jnp.abs(quot(there, size_y).astype(F32) - from_x)
            gx = jnp.minimum(gx, size_x - gx)
            gy = jnp.abs(rest(there, size_y).astype(F32) - from_y)
            gy = jnp.minimum(gy, size_y - gy)
            near = jnp.maximum(1.0 - (gx * gx + gy * gy) * cuts[c], 0.0)
            gain_hi, gain_lo = split2(cross * (near * near))
            heights[c] = hc + (nn(wt_hi, gain_hi) + (nn(wt_hi, gain_lo) + nn(wt_lo, gain_hi)))
            return 0

        lax.fori_loop(b + 1, batches, carry_body, 0)
        return 0

    lax.fori_loop(0, batches, batch_body, 0)


def forecast(ensemble, sea_depth, cutoff, obs, values, variance):
    per, fields, rows, cols = ensemble.shape
    n_mem = lax.axis_size("mem")
    n_sub = lax.axis_size("sub")
    members = per * n_mem
    batches, nobs = obs.shape
    total = batches * nobs
    tiles = cols // LANES
    slot = (per + 1, total // LANES, LANES)
    vmem = pl.BlockSpec(memory_space=pltpu.VMEM)
    hbm = pl.BlockSpec(memory_space=pl.ANY)
    dma = pltpu.SemaphoreType.DMA
    vm = pltpu.VMEM
    return pl.pallas_call(
        forecast_kernel,
        out_shape=(
            jax.ShapeDtypeStruct((n_mem, per, fields, rows, LANES), F32),
            jax.ShapeDtypeStruct((batches, members, nobs), F32),
            jax.ShapeDtypeStruct((batches, members, nobs), F32),
        ),
        in_specs=[hbm, hbm] + [vmem] * 4,
        out_specs=(hbm, vmem, vmem),
        scratch_shapes=[
            vm((per, fields, rows + 2 * HALO, cols), F32),
            vm((rows + 2 * HALO, cols), F32),
            vm((tiles, rows + 4 * HALO, LANES), F32),
            vm((tiles, rows + 4 * HALO, LANES), F32),
            vm((tiles, rows + 2 * HALO, LANES), F32),
            vm((n_sub, *slot), F32),
            vm(slot, F32),
            vm(slot, F32),
            vm((n_mem, *slot), F32),
            vm((tiles, per, fields, rows, LANES), F32),
            vm((members * 8, LANES), F32),
            vm((batches, members, nobs), F32),
            vm((batches, 1, nobs), F32),
            dma((per + 1,)), dma((2, per)), dma((2, per)), dma((2,)), dma((2,)),
            dma((per + 1,)), dma((per + 1,)), dma((per + 1,)), dma((per + 1,)),
            dma((per,)), dma((per,)), dma((per,)),
        ],
        compiler_params=pltpu.CompilerParams(
            collective_id=0, has_side_effects=True, vmem_limit_bytes=56 << 20),
        name="forecast",
    )(ensemble, sea_depth, cutoff, obs, values, variance)


def update_kernel(state_ref, at_hbm, wt_hbm, obs_ref, cut_ref, out_ref,
                  at_ref, wt_ref, lhs1, lhs2, far_x, sq_y, inv_r2, work, begin, stage, counts, in_sems, sems, w_sems):
    members, fields, rows, _ = state_ref.shape
    batches, _, nobs = at_ref.shape
    block = work.shape[2] // (fields * LANES)
    size_x = rows * lax.axis_size("sub")
    size_y = LANES * lax.axis_size("mem")
    x0 = lax.axis_index("sub") * rows
    y0 = lax.axis_index("mem") * LANES

    early = [pltpu.make_async_copy(at_hbm, at_ref, w_sems.at[0]), pltpu.make_async_copy(wt_hbm, wt_ref, w_sems.at[1])]
    for cp in early:
        cp.start()
    for step in range(rows // block):
        pltpu.make_async_copy(
            state_ref.at[:, :, pl.ds(step * block, block)], begin.at[step], in_sems.at[step]).start()
    cut = cut_ref[...].astype(F32)
    inv_r2[...] = 1.0 / (cut * cut)
    top = jnp.max(cut_ref[...])
    reach = top * top
    upper = jnp.where(iota((nobs, nobs), 0) < iota((nobs, nobs), 1), 1.0, 0.0).astype(BF16)

    def gap_to(pos, low, length, size):
        before = low - pos
        before = jnp.where(before < 0, before + size, before)
        after = pos - (low + length - 1)
        after = jnp.where(after < 0, after + size, after)
        inside = (pos >= low) & (pos < low + length)
        return jnp.where(inside, 0, jnp.minimum(before, after))

    def select(b, _):
        ox = quot(obs_ref[pl.ds(b, 1), :], size_y)
        oy = rest(obs_ref[pl.ds(b, 1), :], size_y)
        gx = gap_to(ox, x0, rows, size_x)
        gy = gap_to(oy, y0, LANES, size_y)
        keep = jnp.where(gx * gx + gy * gy < reach, 1.0, 0.0)
        rank = nn(jnp.broadcast_to(keep, (16, nobs)).astype(BF16), upper)[0:1]
        rank = jnp.where(keep > 0.5, rank, -1.0)
        total = jnp.sum(keep).astype(jnp.int32)
        chunks = (total + CHUNK - 1) // CHUNK
        counts[b] = chunks
        a = at_ref[b]
        a_hi, a_lo = split2(a - jnp.mean(a, 0, keepdims=True))
        w_hi, w_lo = split2(wt_ref[b])
        a3 = jnp.concatenate([a_hi, a_hi, a_lo], 0)
        w2 = jnp.concatenate([w_hi, w_lo], 1)

        def pack(c, _):
            want = (iota((CHUNK, nobs), 0) + c * CHUNK).astype(F32)
            hot = jnp.where(rank == want, 1.0, 0.0)
            hot16 = hot.astype(BF16)
            lhs1[b, c] = nt(hot16, a3).astype(BF16)
            zero = jnp.zeros_like(hot16)
            turn = jnp.concatenate(
                [jnp.concatenate([hot16, hot16, zero], 0), jnp.concatenate([zero, zero, hot16], 0)], 1)
            lhs2[b, c] = nt(w2, turn).astype(BF16)
            px = jnp.sum(hot * ox.astype(F32), 1, keepdims=True)
            py = jnp.sum(hot * oy.astype(F32), 1, keepdims=True)
            far_x[b, c] = jnp.broadcast_to(px, (CHUNK, LANES))
            gy = jnp.abs((iota((CHUNK, LANES), 1) + y0).astype(F32) - py)
            gy = jnp.minimum(gy, size_y - gy)
            sq_y[b, c] = gy * gy
            return 0

        lax.fori_loop(0, chunks, pack, 0)
        return 0

    for cp in early:
        cp.wait()
    lax.fori_loop(0, batches, select, 0)

    slabs = fields * block
    steps = rows // block

    def place(s):
        return pl.ds(s % fields * block + s // fields, members, stride=slabs)

    def part(step):
        return pl.ds(pl.multiple_of(step * block, block), block)

    def in_copy(step):
        return pltpu.make_async_copy(state_ref.at[:, :, part(step)], begin.at[step], in_sems.at[step])

    def out_copy(step):
        return pltpu.make_async_copy(stage.at[step], out_ref.at[:, :, part(step)], sems.at[step])

    def step_body(step, _):
        in_copy(step).wait()
        source = begin.at[step].reshape(members * slabs, LANES)
        target = stage.at[step].reshape(members * slabs, LANES)
        for s in range(slabs):
            work[0, :, s * LANES:(s + 1) * LANES] = source[place(s), :]

        def batch_body(b, now):
            chunks = counts[b]

            def chunk_body(c, _):
                left = lhs1[b, c]
                right = lhs2[b, c]
                px = far_x[b, c]
                dy = sq_y[b, c]
                base = jnp.where(c == 0, now, 1 - now)
                for r in range(0, block, GROUP):
                    near = []
                    for k in range(r, r + GROUP):
                        row = step * block + k
                        gx = jnp.abs(px - (x0 + row).astype(F32))
                        gx = jnp.minimum(gx, size_x - gx)
                        ratio = (gx * gx + dy) * inv_r2[pl.ds(row, 1), :]
                        part = jnp.maximum(1.0 - ratio, 0.0)
                        near += [part * part] * fields
                    near = jnp.concatenate(near, 1)
                    span = slice(r * fields * LANES, (r + GROUP) * fields * LANES)
                    hi, lo = split2(work[now, :, span])
                    hi, lo = split2(nn(left, jnp.concatenate([hi, lo, hi], 0)) * near)
                    work[1 - now, :, span] = work[base, :, span] + nn(right, jnp.concatenate([hi, lo, hi], 0))
                return 0

            lax.fori_loop(0, chunks, chunk_body, 0)
            return jnp.where(chunks > 0, 1 - now, now)

        last = lax.fori_loop(0, batches, batch_body, 0)
        for s in range(slabs):
            target[place(s), :] = work[last, :, s * LANES:(s + 1) * LANES]
        out_copy(step).start()
        return 0

    lax.fori_loop(0, steps, step_body, 0)
    for step in range(steps):
        out_copy(step).wait()


def update(state, at, wt, obs, cutoff):
    members, fields, rows, _ = state.shape
    batches, _, nobs = at.shape
    block = 8
    chunks = nobs // CHUNK
    vmem = pl.BlockSpec(memory_space=pltpu.VMEM)
    width = fields * block * LANES
    return pl.pallas_call(
        update_kernel,
        out_shape=jax.ShapeDtypeStruct(state.shape, F32),
        in_specs=[pl.BlockSpec(memory_space=pl.ANY)] * 3 + [vmem] * 2,
        out_specs=pl.BlockSpec(memory_space=pl.ANY),
        scratch_shapes=[
            pltpu.VMEM(at.shape, F32),
            pltpu.VMEM(wt.shape, F32),
            pltpu.VMEM((batches, chunks, CHUNK, 3 * members), BF16),
            pltpu.VMEM((batches, chunks, members, 3 * CHUNK), BF16),
            pltpu.VMEM((batches, chunks, CHUNK, LANES), F32),
            pltpu.VMEM((batches, chunks, CHUNK, LANES), F32),
            pltpu.VMEM((rows, LANES), F32),
            pltpu.VMEM((2, members, width), F32),
            pltpu.VMEM((rows // block, members, fields, block, LANES), F32),
            pltpu.VMEM((rows // block, members, fields, block, LANES), F32),
            pltpu.SMEM((batches,), jnp.int32),
            pltpu.SemaphoreType.DMA((rows // block,)),
            pltpu.SemaphoreType.DMA((rows // block,)),
            pltpu.SemaphoreType.DMA((2,)),
        ],
        compiler_params=pltpu.CompilerParams(vmem_limit_bytes=63 << 20),
        name="update",
    )(state, at, wt, obs, cutoff)


def local(ensemble, sea_depth, cutoff, obs_index, obs_value, obs_var):
    per, fields, rows, cols = ensemble.shape
    members = per * lax.axis_size("mem")
    state, at, wt = forecast(ensemble, sea_depth, cutoff, obs_index, obs_value, obs_var)
    return update(state.reshape(members, fields, rows, LANES), at, wt, obs_index, cutoff)


def solution(mesh):
    return jax.shard_map(
        local,
        mesh=mesh,
        in_specs=(P("mem", None, "sub", None), P("sub", None), P("sub", "mem"), P(), P(), P()),
        out_specs=P(None, None, "sub", "mem"),
        check_vma=False,
    )
```

```python
import functools

import jax
import jax.numpy as jnp
from jax import lax
from jax.experimental import pallas as pl
from jax.experimental.pallas import tpu as pltpu
from jax.sharding import PartitionSpec as P

STEPS = 4
BATCHES = 4
DT = 0.3
CORIOLIS = 0.2
MESH = pl.DeviceIdType.MESH
HIGHEST = lax.Precision.HIGHEST
F32 = jnp.float32
BF16 = jnp.bfloat16
HALO = 8
CHUNK = 40
GROUP = 8
LANES = 128


def nt(a, b, precision=None):
    return lax.dot_general(
        a, b, (((1,), (1,)), ((), ())), precision=precision, preferred_element_type=F32
    )


def nn(a, b, precision=None):
    return lax.dot_general(
        a, b, (((1,), (0,)), ((), ())), precision=precision, preferred_element_type=F32
    )


def split2(x):
    hi = x.astype(BF16)
    return hi, (x - hi.astype(F32)).astype(BF16)


def quot(x, size):
    return x >> (size.bit_length() - 1)


def rest(x, size):
    return x & (size - 1)


def iota(shape, dim):
    return lax.broadcasted_iota(jnp.int32, shape, dim)


SIDE = 4
ORDER = (
    (0, 1), (0, 3), (1, 0), (3, 0), (1, 1), (3, 3), (1, 3), (3, 1),
    (0, 2), (2, 0), (2, 1), (2, 3), (1, 2), (3, 2), (2, 2),
)
EARLY = 2
SOME = 5


def forecast_kernel(
    ens_ref, depth_ref, cut_ref, obs_ref, val_ref, var_ref,
    out_ref, at_ref, wt_ref,
    ext, dep, hbuf, fbuf, gbuf, part, slots, mine, prior_ref, staged, flat, heights, cuts,
    lsem, hs_sem, hr_sem, ds_sem, dr_sem, s1_sem, r1_sem, s2_sem, r2_sem, bs_sem, br_sem, own_sem,
):
    members, fields, rows, cols = ens_ref.shape
    tiles = cols // LANES
    me = lax.axis_index("mem")
    sub = lax.axis_index("sub")
    n_mem = lax.axis_size("mem")
    n_sub = lax.axis_size("sub")
    nobs = obs_ref.shape[0] * obs_ref.shape[1]

    barrier = pltpu.get_barrier_semaphore()
    for k in range(1, n_sub):
        pl.semaphore_signal(barrier, inc=1, device_id=(me, lax.rem(sub + k, n_sub)), device_id_type=MESH)
    for k in range(1, n_mem):
        pl.semaphore_signal(barrier, inc=1, device_id=(lax.rem(me + k, n_mem), sub), device_id_type=MESH)

    local = []
    cp = pltpu.make_async_copy(depth_ref, dep.at[pl.ds(HALO, rows)], lsem.at[members])
    cp.start()
    local.append(cp)
    for m in range(members):
        cp = pltpu.make_async_copy(ens_ref.at[m], ext.at[m, :, pl.ds(HALO, rows)], lsem.at[m])
        cp.start()
        local.append(cp)
    pl.semaphore_wait(barrier, n_sub - 1 + n_mem - 1)

    up = lax.rem(sub + n_sub - 1, n_sub)
    down = lax.rem(sub + 1, n_sub)
    halo = []
    for d, (peer, src, dst) in enumerate(((up, 0, HALO + rows), (down, rows - HALO, 0))):
        cp = pltpu.make_async_remote_copy(
            depth_ref.at[pl.ds(src, HALO)], dep.at[pl.ds(dst, HALO)],
            ds_sem.at[d], dr_sem.at[d], device_id=(me, peer), device_id_type=MESH)
        cp.start()
        halo.append(cp)

    def halo_copies(m):
        return [
            pltpu.make_async_remote_copy(
                ens_ref.at[m, :, pl.ds(src, HALO)], ext.at[m, :, pl.ds(dst, HALO)],
                hs_sem.at[d, m], hr_sem.at[d, m], device_id=(me, peer), device_id_type=MESH)
            for d, (peer, src, dst) in enumerate(((up, 0, HALO + rows), (down, rows - HALO, 0)))
        ]

    for m in range(members):
        for cp in halo_copies(m):
            cp.start()

    index = jnp.concatenate([obs_ref[b:b + 1, :] for b in range(obs_ref.shape[0])], 1)
    obs_x = quot(index, cols)
    obs_y = rest(index, cols)
    local_x = obs_x - sub * rows
    in_rows = (local_x >= 0) & (local_x < rows)
    combo = jnp.where(in_rows, quot(obs_y, LANES) * rows + local_x, -1)
    lane_of = rest(obs_y, LANES)

    in_block = in_rows & (quot(obs_y, LANES) == me)
    pick_row = jnp.where(in_block, local_x, -1)
    cut_t = jnp.transpose(cut_ref[...].astype(F32))
    row_hot = jnp.where(iota((rows, nobs), 0) == pick_row, 1.0, 0.0)
    cut_cols = nn(cut_t.astype(BF16), row_hot.astype(BF16))
    cut_obs = jnp.sum(jnp.where(iota((LANES, nobs), 0) == lane_of, cut_cols, 0.0), 0, keepdims=True)
    for q in range(nobs // LANES):
        mine[0, q:q + 1, :] = cut_obs[:, q * LANES:(q + 1) * LANES]

    def send_part(s):
        part[sub, s] = mine[s]
        for k in range(1, n_sub):
            pltpu.make_async_remote_copy(
                mine.at[s], part.at[sub, s], s1_sem.at[s], r1_sem.at[s],
                device_id=(me, lax.rem(sub + k, n_sub)), device_id_type=MESH).start()

    def send_total(s):
        all_parts = part.at[pl.ds(0, n_sub - 1), s]
        pltpu.make_async_copy(all_parts, all_parts, r1_sem.at[s]).wait()
        total = part[0, s]
        for k in range(1, n_sub):
            total = total + part[k, s]
        slots[s] = total
        prior_ref[me, s] = total
        for k in range(1, n_mem):
            pltpu.make_async_remote_copy(
                slots.at[s], prior_ref.at[me, s], s2_sem.at[s], r2_sem.at[s],
                device_id=(lax.rem(me + k, n_mem), sub), device_id_type=MESH).start()

    send_part(0)

    halo[0].wait()
    halo[1].wait()
    local[0].wait()

    height = rows + 2 * HALO
    lane = iota((height, LANES), 1)
    here, above, below = (pl.ds(HALO + k, height) for k in (0, 1, -1))
    pad = jnp.zeros((HALO, LANES), F32)
    for buf in (hbuf, fbuf):
        for t in range(tiles):
            buf[t, 0:HALO] = pad
            buf[t, HALO + height:] = pad

    def cols_of(t):
        return pl.ds(t * LANES, LANES)

    def spread(load, lane):
        first_east = pltpu.roll(load(0), LANES - 1, 1)
        east = first_east
        west_before = pltpu.roll(load(tiles - 1), 1, 1)
        for t in range(tiles):
            east_next = first_east if t == tiles - 1 else pltpu.roll(load(t + 1), LANES - 1, 1)
            west = pltpu.roll(load(t), 1, 1)
            yield t, jnp.where(lane < LANES - 1, east, east_next) - jnp.where(lane > 0, west, west_before)
            east, west_before = east_next, west

    half = 0.5 * DT

    def block_copies(m, first, last):
        found = []
        for n, (dz, dx) in list(enumerate(ORDER))[first:last]:
            peer = lax.rem(me // SIDE + dz, SIDE) * SIDE + lax.rem(lax.rem(me, SIDE) + dx, SIDE)
            found.append(pltpu.make_async_remote_copy(
                staged.at[peer, m], out_ref.at[me, m], bs_sem.at[m], br_sem.at[m],
                device_id=(peer, sub), device_id_type=MESH))
        return found

    def own_copy(m):
        return pltpu.make_async_copy(staged.at[me, m], out_ref.at[me, m], own_sem.at[m])

    def member_body(m, _):
        pltpu.make_async_copy(ens_ref.at[m], ext.at[m, :, pl.ds(HALO, rows)], lsem.at[m]).wait()
        for cp in halo_copies(m):
            cp.wait()
        for t in range(tiles):
            hbuf[t, here] = ext[m, 0, :, cols_of(t)]

        def step_body(s, carry):
            for t, h_dy in spread(lambda t: hbuf[t, here], lane):
                u = ext[m, 1, :, cols_of(t)]
                v = ext[m, 2, :, cols_of(t)]
                u1 = u + ((DT * CORIOLIS) * v - half * (hbuf[t, above] - hbuf[t, below]))
                v1 = v - ((DT * CORIOLIS) * u + half * h_dy)
                d = dep[:, cols_of(t)]
                ext[m, 1, :, cols_of(t)] = u1
                ext[m, 2, :, cols_of(t)] = v1
                fbuf[t, here] = d * u1
                gbuf[t] = d * v1
            for t, g_dy in spread(lambda t: gbuf[t], lane):
                hbuf[t, here] = hbuf[t, here] - half * (fbuf[t, above] - fbuf[t, below] + g_dy)
            return carry

        lax.fori_loop(0, STEPS - 1, step_body, 0)
        inner = pl.ds(2 * HALO, rows)
        north, south = pl.ds(2 * HALO + 1, rows), pl.ds(2 * HALO - 1, rows)
        own = pl.ds(HALO, rows)
        for t, h_dy in spread(lambda t: hbuf[t, inner], lane[:rows]):
            u = ext[m, 1, :, cols_of(t)]
            v = ext[m, 2, :, cols_of(t)]
            u1 = u + ((DT * CORIOLIS) * v - half * (hbuf[t, above] - hbuf[t, below]))
            v1 = v[HALO:HALO + rows] - ((DT * CORIOLIS) * u[HALO:HALO + rows] + half * h_dy)
            d = dep[:, cols_of(t)]
            staged[t, m, 1] = u1[HALO:HALO + rows]
            staged[t, m, 2] = v1
            fbuf[t, here] = d * u1
            gbuf[t, own] = d[HALO:HALO + rows] * v1
        for t, g_dy in spread(lambda t: gbuf[t, own], lane[:rows]):
            staged[t, m, 0] = hbuf[t, inner] - half * (fbuf[t, north] - fbuf[t, south] + g_dy)
        own_copy(m).start()

        @pl.when(m < EARLY)
        def _():
            for cp in block_copies(m, 0, len(ORDER)):
                cp.start()

        @pl.when(m == EARLY)
        def _():
            for cp in block_copies(m, 0, SOME):
                cp.start()

        send_total(m)
        block = 256
        turned = jnp.concatenate(
            [jnp.transpose(jnp.concatenate([staged[t, m, 0] for t in range(4 * g, 4 * g + 4)], 0))
             for g in range(tiles // 4)], 1)
        parts = jnp.concatenate(split2(turned), 0)
        for q in range(nobs // block):
            span = slice(q * block, (q + 1) * block)
            hot = jnp.where(iota((tiles * rows, block), 0) == combo[:, span], 1.0, 0.0).astype(BF16)
            picked = nn(parts, hot)
            picked = picked[0:LANES] + picked[LANES:]
            got = jnp.sum(jnp.where(iota((LANES, block), 0) == lane_of[:, span], picked, 0.0), 0, keepdims=True)
            for s in range(block // LANES):
                mine[m + 1, pl.ds(q * (block // LANES) + s, 1), :] = got[:, s * LANES:(s + 1) * LANES]
        send_part(m + 1)
        return 0

    lax.fori_loop(0, members, member_body, 0)

    send_total(members)

    for cp in block_copies(EARLY, SOME, len(ORDER)):
        cp.start()

    def rest_body(m, _):
        for cp in block_copies(m, 0, len(ORDER)):
            cp.start()
        return 0

    lax.fori_loop(EARLY + 1, members, rest_body, 0)
    def totals_body(s, _):
        for sent, sems, count in ((part, s1_sem, n_sub), (prior_ref, s2_sem, n_mem), (prior_ref, r2_sem, n_mem)):
            peers = sent.at[pl.ds(0, count - 1), s]
            pltpu.make_async_copy(peers, peers, sems.at[s]).wait()
        return 0

    lax.fori_loop(0, members + 1, totals_body, 0)
    weights(prior_ref, obs_ref, val_ref, var_ref, at_ref, wt_ref, flat, heights, cuts,
            rows * n_sub, cols)

    def finish_body(m, _):
        peers = out_ref.at[pl.ds(0, n_mem - 1), m]
        for sems in (bs_sem, br_sem):
            pltpu.make_async_copy(peers, peers, sems.at[m]).wait()
        own_copy(m).wait()
        return 0

    lax.fori_loop(0, members, finish_body, 0)


def nn3(a, b):
    a_hi, a_lo = split2(a)
    b_hi, b_lo = split2(b)
    return nn(a_hi, b_hi) + (nn(a_hi, b_lo) + nn(a_lo, b_hi))


def weights(prior_ref, obs_ref, val_ref, var_ref, at_ref, wt_ref, flat, heights, cuts, size_x, size_y):
    n_mem, width, _, _ = prior_ref.shape
    batches, members, nobs = at_ref.shape
    groups = batches * nobs // LANES
    flat[...] = prior_ref[:, 1:].reshape(members * 8, LANES)
    cut = jnp.sum(prior_ref[:, 0], 0)
    cut = 1.0 / (cut * cut)
    for q in range(groups):
        b, s = q * LANES // nobs, q * LANES % nobs
        heights[b, :, s:s + LANES] = flat[pl.ds(q, members, stride=8), :]
        cuts[b, :, s:s + LANES] = cut[q:q + 1, :]
    scale = 1.0 / (members - 1)

    def batch_body(b, _):
        h = heights[b]
        mean = jnp.mean(h, 0, keepdims=True)
        at = h - mean
        inv_var = 1.0 / var_ref[pl.ds(b, 1), :]
        scaled = at * inv_var
        gram = nt(scaled, at, HIGHEST) * scale
        eye = jnp.where(iota((members, members), 0) == iota((members, members), 1), 1.0, 0.0)
        x = jnp.concatenate([eye, gram + eye], 1)
        line = iota(x.shape, 0)
        for k in range(0, members, 8):
            ahead = [jnp.broadcast_to(x[:, members + k + l:members + k + l + 1], x.shape) for l in range(8)]
            for j in range(0, 8, 2):
                p, q = k + j, k + j + 1
                col0, col1 = ahead[0], ahead[1]
                a, b01, c = col0[p:p + 1], col1[p:p + 1], col1[q:q + 1]
                inv = 1.0 / (a * c - b01 * b01)
                a, b01, c = a * inv, b01 * inv, c * inv

                def sweep(y):
                    row0 = c * y[p:p + 1] - b01 * y[q:q + 1]
                    row1 = a * y[q:q + 1] - b01 * y[p:p + 1]
                    left = y - col0 * row0 - col1 * row1
                    return jnp.where(line == p, row0, jnp.where(line == q, row1, left))

                ahead = [sweep(y) for y in ahead[2:]]
                x = sweep(x)
        inverse = x[:, 0:members]
        big = nn3(inverse, scaled)
        gap = (val_ref[pl.ds(b, 1), :] - mean) * inv_var
        lean = jnp.sum(at * gap, 1, keepdims=True)
        small = gap - scale * jnp.sum(big * lean, 0, keepdims=True)
        wt = small - 0.5 * big
        at_ref[b] = at * scale
        wt_ref[b] = wt

        here = obs_ref[pl.ds(b, 1), :]
        xy = jnp.concatenate(
            [jnp.broadcast_to(k.astype(F32), (4, nobs)) for k in (quot(here, size_y), rest(here, size_y))], 0)
        xy = jnp.transpose(xy)
        from_x = xy[:, 0:1]
        from_y = xy[:, 4:5]
        anom_hi, anom_lo = split2(jnp.transpose(at * scale))
        wt_hi, wt_lo = split2(wt)

        def carry_body(c, _):
            hc = heights[c]
            dev_hi, dev_lo = split2(hc - jnp.mean(hc, 0, keepdims=True))
            cross = nn(anom_hi, dev_hi) + (nn(anom_hi, dev_lo) + nn(anom_lo, dev_hi))
            there = obs_ref[pl.ds(c, 1), :]
            gx = jnp.abs(quot(there, size_y).astype(F32) - from_x)
            gx = jnp.minimum(gx, size_x - gx)
            gy = jnp.abs(rest(there, size_y).astype(F32) - from_y)
            gy = jnp.minimum(gy, size_y - gy)
            near = jnp.maximum(1.0 - (gx * gx + gy * gy) * cuts[c], 0.0)
            gain_hi, gain_lo = split2(cross * (near * near))
            heights[c] = hc + (nn(wt_hi, gain_hi) + (nn(wt_hi, gain_lo) + nn(wt_lo, gain_hi)))
            return 0

        lax.fori_loop(b + 1, batches, carry_body, 0)
        return 0

    lax.fori_loop(0, batches, batch_body, 0)


def forecast(ensemble, sea_depth, cutoff, obs, values, variance):
    per, fields, rows, cols = ensemble.shape
    n_mem = lax.axis_size("mem")
    n_sub = lax.axis_size("sub")
    members = per * n_mem
    batches, nobs = obs.shape
    total = batches * nobs
    tiles = cols // LANES
    slot = (per + 1, total // LANES, LANES)
    vmem = pl.BlockSpec(memory_space=pltpu.VMEM)
    hbm = pl.BlockSpec(memory_space=pl.ANY)
    dma = pltpu.SemaphoreType.DMA
    vm = pltpu.VMEM
    return pl.pallas_call(
        forecast_kernel,
        out_shape=(
            jax.ShapeDtypeStruct((n_mem, per, fields, rows, LANES), F32),
            jax.ShapeDtypeStruct((batches, members, nobs), F32),
            jax.ShapeDtypeStruct((batches, members, nobs), F32),
        ),
        in_specs=[hbm, hbm] + [vmem] * 4,
        out_specs=(hbm, vmem, vmem),
        scratch_shapes=[
            vm((per, fields, rows + 2 * HALO, cols), F32),
            vm((rows + 2 * HALO, cols), F32),
            vm((tiles, rows + 4 * HALO, LANES), F32),
            vm((tiles, rows + 4 * HALO, LANES), F32),
            vm((tiles, rows + 2 * HALO, LANES), F32),
            vm((n_sub, *slot), F32),
            vm(slot, F32),
            vm(slot, F32),
            vm((n_mem, *slot), F32),
            vm((tiles, per, fields, rows, LANES), F32),
            vm((members * 8, LANES), F32),
            vm((batches, members, nobs), F32),
            vm((batches, 1, nobs), F32),
            dma((per + 1,)), dma((2, per)), dma((2, per)), dma((2,)), dma((2,)),
            dma((per + 1,)), dma((per + 1,)), dma((per + 1,)), dma((per + 1,)),
            dma((per,)), dma((per,)), dma((per,)),
        ],
        compiler_params=pltpu.CompilerParams(
            collective_id=0, has_side_effects=True, vmem_limit_bytes=56 << 20),
        name="forecast",
    )(ensemble, sea_depth, cutoff, obs, values, variance)


def update_kernel(state_ref, at_hbm, wt_hbm, obs_ref, cut_ref, out_ref,
                  at_ref, wt_ref, lhs1, lhs2, far_x, sq_y, inv_r2, work, begin, stage, counts, in_sems, sems, w_sems):
    members, fields, rows, _ = state_ref.shape
    batches, _, nobs = at_ref.shape
    block = work.shape[2] // (fields * LANES)
    size_x = rows * lax.axis_size("sub")
    size_y = LANES * lax.axis_size("mem")
    x0 = lax.axis_index("sub") * rows
    y0 = lax.axis_index("mem") * LANES

    early = [pltpu.make_async_copy(at_hbm, at_ref, w_sems.at[0]), pltpu.make_async_copy(wt_hbm, wt_ref, w_sems.at[1])]
    for cp in early:
        cp.start()
    for step in range(rows // block):
        pltpu.make_async_copy(
            state_ref.at[:, :, pl.ds(step * block, block)], begin.at[step], in_sems.at[step]).start()
    cut = cut_ref[...].astype(F32)
    inv_r2[...] = 1.0 / (cut * cut)
    top = jnp.max(cut_ref[...])
    reach = top * top
    upper = jnp.where(iota((nobs, nobs), 0) < iota((nobs, nobs), 1), 1.0, 0.0).astype(BF16)

    def gap_to(pos, low, length, size):
        before = low - pos
        before = jnp.where(before < 0, before + size, before)
        after = pos - (low + length - 1)
        after = jnp.where(after < 0, after + size, after)
        inside = (pos >= low) & (pos < low + length)
        return jnp.where(inside, 0, jnp.minimum(before, after))

    def select(b, _):
        ox = quot(obs_ref[pl.ds(b, 1), :], size_y)
        oy = rest(obs_ref[pl.ds(b, 1), :], size_y)
        gx = gap_to(ox, x0, rows, size_x)
        gy = gap_to(oy, y0, LANES, size_y)
        keep = jnp.where(gx * gx + gy * gy < reach, 1.0, 0.0)
        rank = nn(jnp.broadcast_to(keep, (16, nobs)).astype(BF16), upper)[0:1]
        rank = jnp.where(keep > 0.5, rank, -1.0)
        total = jnp.sum(keep).astype(jnp.int32)
        chunks = (total + CHUNK - 1) // CHUNK
        counts[b] = chunks
        a = at_ref[b]
        a_hi, a_lo = split2(a - jnp.mean(a, 0, keepdims=True))
        w_hi, w_lo = split2(wt_ref[b])
        a3 = jnp.concatenate([a_hi, a_hi, a_lo], 0)
        w2 = jnp.concatenate([w_hi, w_lo], 1)

        def pack(c, _):
            want = (iota((CHUNK, nobs), 0) + c * CHUNK).astype(F32)
            hot = jnp.where(rank == want, 1.0, 0.0)
            hot16 = hot.astype(BF16)
            lhs1[b, c] = nt(hot16, a3).astype(BF16)
            zero = jnp.zeros_like(hot)
            turn = jnp.concatenate(
                [jnp.concatenate([hot, hot, zero], 0), jnp.concatenate([zero, zero, hot], 0)], 1).astype(BF16)
            lhs2[b, c] = nt(w2, turn).astype(BF16)
            px = jnp.sum(hot * ox.astype(F32), 1, keepdims=True)
            py = jnp.sum(hot * oy.astype(F32), 1, keepdims=True)
            far_x[b, c] = jnp.broadcast_to(px, (CHUNK, LANES))
            gy = jnp.abs((iota((CHUNK, LANES), 1) + y0).astype(F32) - py)
            gy = jnp.minimum(gy, size_y - gy)
            sq_y[b, c] = gy * gy
            return 0

        lax.fori_loop(0, chunks, pack, 0)
        return 0

    for cp in early:
        cp.wait()
    lax.fori_loop(0, batches, select, 0)

    slabs = fields * block
    steps = rows // block

    def place(s):
        return pl.ds(s % fields * block + s // fields, members, stride=slabs)

    def part(step):
        return pl.ds(pl.multiple_of(step * block, block), block)

    def in_copy(step):
        return pltpu.make_async_copy(state_ref.at[:, :, part(step)], begin.at[step], in_sems.at[step])

    def out_copy(step):
        return pltpu.make_async_copy(stage.at[step], out_ref.at[:, :, part(step)], sems.at[step])

    def step_body(step, _):
        in_copy(step).wait()
        source = begin.at[step].reshape(members * slabs, LANES)
        target = stage.at[step].reshape(members * slabs, LANES)
        for s in range(slabs):
            work[0, :, s * LANES:(s + 1) * LANES] = source[place(s), :]

        def batch_body(b, now):
            chunks = counts[b]

            def chunk_body(c, _):
                left = lhs1[b, c]
                right = lhs2[b, c]
                px = far_x[b, c]
                dy = sq_y[b, c]
                base = jnp.where(c == 0, now, 1 - now)
                for r in range(0, block, GROUP):
                    near = []
                    for k in range(r, r + GROUP):
                        row = step * block + k
                        gx = jnp.abs(px - (x0 + row).astype(F32))
                        gx = jnp.minimum(gx, size_x - gx)
                        ratio = (gx * gx + dy) * inv_r2[pl.ds(row, 1), :]
                        part = jnp.maximum(1.0 - ratio, 0.0)
                        near += [part * part] * fields
                    near = jnp.concatenate(near, 1)
                    span = slice(r * fields * LANES, (r + GROUP) * fields * LANES)
                    hi, lo = split2(work[now, :, span])
                    gain = nn(left, jnp.concatenate([hi, lo, hi], 0)) * near
                    top = gain.astype(BF16).astype(F32)
                    stacked = jnp.concatenate([top, gain - top, top], 0).astype(BF16)
                    work[1 - now, :, span] = work[base, :, span] + nn(right, stacked)
                return 0

            lax.fori_loop(0, chunks, chunk_body, 0)
            return jnp.where(chunks > 0, 1 - now, now)

        last = lax.fori_loop(0, batches, batch_body, 0)
        for s in range(slabs):
            target[place(s), :] = work[last, :, s * LANES:(s + 1) * LANES]
        out_copy(step).start()
        return 0

    lax.fori_loop(0, steps, step_body, 0)
    for step in range(steps):
        out_copy(step).wait()


def update(state, at, wt, obs, cutoff):
    members, fields, rows, _ = state.shape
    batches, _, nobs = at.shape
    block = 8
    chunks = pl.cdiv(nobs, CHUNK)
    vmem = pl.BlockSpec(memory_space=pltpu.VMEM)
    width = fields * block * LANES
    return pl.pallas_call(
        update_kernel,
        out_shape=jax.ShapeDtypeStruct(state.shape, F32),
        in_specs=[pl.BlockSpec(memory_space=pl.ANY)] * 3 + [vmem] * 2,
        out_specs=pl.BlockSpec(memory_space=pl.ANY),
        scratch_shapes=[
            pltpu.VMEM(at.shape, F32),
            pltpu.VMEM(wt.shape, F32),
            pltpu.VMEM((batches, chunks, CHUNK, 3 * members), BF16),
            pltpu.VMEM((batches, chunks, members, 3 * CHUNK), BF16),
            pltpu.VMEM((batches, chunks, CHUNK, LANES), F32),
            pltpu.VMEM((batches, chunks, CHUNK, LANES), F32),
            pltpu.VMEM((rows, LANES), F32),
            pltpu.VMEM((2, members, width), F32),
            pltpu.VMEM((rows // block, members, fields, block, LANES), F32),
            pltpu.VMEM((rows // block, members, fields, block, LANES), F32),
            pltpu.SMEM((batches,), jnp.int32),
            pltpu.SemaphoreType.DMA((rows // block,)),
            pltpu.SemaphoreType.DMA((rows // block,)),
            pltpu.SemaphoreType.DMA((2,)),
        ],
        compiler_params=pltpu.CompilerParams(vmem_limit_bytes=63 << 20),
        name="update",
    )(state, at, wt, obs, cutoff)


def local(ensemble, sea_depth, cutoff, obs_index, obs_value, obs_var):
    per, fields, rows, cols = ensemble.shape
    members = per * lax.axis_size("mem")
    state, at, wt = forecast(ensemble, sea_depth, cutoff, obs_index, obs_value, obs_var)
    return update(state.reshape(members, fields, rows, LANES), at, wt, obs_index, cutoff)


def solution(mesh):
    return jax.shard_map(
        local,
        mesh=mesh,
        in_specs=(P("mem", None, "sub", None), P("sub", None), P("sub", "mem"), P(), P(), P()),
        out_specs=P(None, None, "sub", "mem"),
        check_vma=False,
    )
```

```python
import functools

import jax
import jax.numpy as jnp
from jax import lax
from jax.experimental import pallas as pl
from jax.experimental.pallas import tpu as pltpu
from jax.sharding import PartitionSpec as P

STEPS = 4
BATCHES = 4
DT = 0.3
CORIOLIS = 0.2
MESH = pl.DeviceIdType.MESH
HIGHEST = lax.Precision.HIGHEST
F32 = jnp.float32
BF16 = jnp.bfloat16
HALO = 8
CHUNK = 40
GROUP = 8
LANES = 128


def nt(a, b, precision=None):
    return lax.dot_general(
        a, b, (((1,), (1,)), ((), ())), precision=precision, preferred_element_type=F32
    )


def nn(a, b, precision=None):
    return lax.dot_general(
        a, b, (((1,), (0,)), ((), ())), precision=precision, preferred_element_type=F32
    )


def split2(x):
    hi = x.astype(BF16)
    return hi, (x - hi.astype(F32)).astype(BF16)


def quot(x, size):
    return x >> (size.bit_length() - 1)


def rest(x, size):
    return x & (size - 1)


def iota(shape, dim):
    return lax.broadcasted_iota(jnp.int32, shape, dim)


SIDE = 4
ORDER = (
    (0, 1), (0, 3), (1, 0), (3, 0), (1, 1), (3, 3), (1, 3), (3, 1),
    (0, 2), (2, 0), (2, 1), (2, 3), (1, 2), (3, 2), (2, 2),
)
EARLY = 2
SOME = 8


def forecast_kernel(
    ens_ref, depth_ref, cut_ref, obs_ref, val_ref, var_ref,
    out_ref, at_ref, wt_ref,
    ext, dep, hbuf, fbuf, gbuf, part, slots, mine, prior_ref, staged, flat, heights, cuts,
    lsem, hs_sem, hr_sem, ds_sem, dr_sem, s1_sem, r1_sem, s2_sem, r2_sem, bs_sem, br_sem, own_sem,
):
    members, fields, rows, cols = ens_ref.shape
    tiles = cols // LANES
    me = lax.axis_index("mem")
    sub = lax.axis_index("sub")
    n_mem = lax.axis_size("mem")
    n_sub = lax.axis_size("sub")
    nobs = obs_ref.shape[0] * obs_ref.shape[1]

    barrier = pltpu.get_barrier_semaphore()
    for k in range(1, n_sub):
        pl.semaphore_signal(barrier, inc=1, device_id=(me, lax.rem(sub + k, n_sub)), device_id_type=MESH)
    for k in range(1, n_mem):
        pl.semaphore_signal(barrier, inc=1, device_id=(lax.rem(me + k, n_mem), sub), device_id_type=MESH)

    local = []
    cp = pltpu.make_async_copy(depth_ref, dep.at[pl.ds(HALO, rows)], lsem.at[members])
    cp.start()
    local.append(cp)
    for m in range(members):
        cp = pltpu.make_async_copy(ens_ref.at[m], ext.at[m, :, pl.ds(HALO, rows)], lsem.at[m])
        cp.start()
        local.append(cp)
    pl.semaphore_wait(barrier, n_sub - 1 + n_mem - 1)

    up = lax.rem(sub + n_sub - 1, n_sub)
    down = lax.rem(sub + 1, n_sub)
    halo = []
    for d, (peer, src, dst) in enumerate(((up, 0, HALO + rows), (down, rows - HALO, 0))):
        cp = pltpu.make_async_remote_copy(
            depth_ref.at[pl.ds(src, HALO)], dep.at[pl.ds(dst, HALO)],
            ds_sem.at[d], dr_sem.at[d], device_id=(me, peer), device_id_type=MESH)
        cp.start()
        halo.append(cp)

    def halo_copies(m):
        return [
            pltpu.make_async_remote_copy(
                ens_ref.at[m, :, pl.ds(src, HALO)], ext.at[m, :, pl.ds(dst, HALO)],
                hs_sem.at[d, m], hr_sem.at[d, m], device_id=(me, peer), device_id_type=MESH)
            for d, (peer, src, dst) in enumerate(((up, 0, HALO + rows), (down, rows - HALO, 0)))
        ]

    for m in range(members):
        for cp in halo_copies(m):
            cp.start()

    index = jnp.concatenate([obs_ref[b:b + 1, :] for b in range(obs_ref.shape[0])], 1)
    obs_x = quot(index, cols)
    obs_y = rest(index, cols)
    local_x = obs_x - sub * rows
    in_rows = (local_x >= 0) & (local_x < rows)
    combo = jnp.where(in_rows, quot(obs_y, LANES) * rows + local_x, -1)
    lane_of = rest(obs_y, LANES)

    in_block = in_rows & (quot(obs_y, LANES) == me)
    pick_row = jnp.where(in_block, local_x, -1)
    cut_t = jnp.transpose(cut_ref[...].astype(F32))
    row_hot = jnp.where(iota((rows, nobs), 0) == pick_row, 1.0, 0.0)
    cut_cols = nn(cut_t.astype(BF16), row_hot.astype(BF16))
    cut_obs = jnp.sum(jnp.where(iota((LANES, nobs), 0) == lane_of, cut_cols, 0.0), 0, keepdims=True)
    for q in range(nobs // LANES):
        mine[0, q:q + 1, :] = cut_obs[:, q * LANES:(q + 1) * LANES]

    def send_part(s):
        part[sub, s] = mine[s]
        for k in range(1, n_sub):
            pltpu.make_async_remote_copy(
                mine.at[s], part.at[sub, s], s1_sem.at[s], r1_sem.at[s],
                device_id=(me, lax.rem(sub + k, n_sub)), device_id_type=MESH).start()

    def send_total(s):
        all_parts = part.at[pl.ds(0, n_sub - 1), s]
        pltpu.make_async_copy(all_parts, all_parts, r1_sem.at[s]).wait()
        total = part[0, s]
        for k in range(1, n_sub):
            total = total + part[k, s]
        slots[s] = total
        prior_ref[me, s] = total
        for k in range(1, n_mem):
            pltpu.make_async_remote_copy(
                slots.at[s], prior_ref.at[me, s], s2_sem.at[s], r2_sem.at[s],
                device_id=(lax.rem(me + k, n_mem), sub), device_id_type=MESH).start()

    send_part(0)

    halo[0].wait()
    halo[1].wait()
    local[0].wait()

    height = rows + 2 * HALO
    lane = iota((height, LANES), 1)
    here, above, below = (pl.ds(HALO + k, height) for k in (0, 1, -1))
    pad = jnp.zeros((HALO, LANES), F32)
    for buf in (hbuf, fbuf):
        for t in range(tiles):
            buf[t, 0:HALO] = pad
            buf[t, HALO + height:] = pad

    def cols_of(t):
        return pl.ds(t * LANES, LANES)

    def spread(load, lane):
        first_east = pltpu.roll(load(0), LANES - 1, 1)
        east = first_east
        west_before = pltpu.roll(load(tiles - 1), 1, 1)
        for t in range(tiles):
            east_next = first_east if t == tiles - 1 else pltpu.roll(load(t + 1), LANES - 1, 1)
            west = pltpu.roll(load(t), 1, 1)
            yield t, jnp.where(lane < LANES - 1, east, east_next) - jnp.where(lane > 0, west, west_before)
            east, west_before = east_next, west

    half = 0.5 * DT

    def block_copies(m, first, last):
        found = []
        for n, (dz, dx) in list(enumerate(ORDER))[first:last]:
            peer = lax.rem(me // SIDE + dz, SIDE) * SIDE + lax.rem(lax.rem(me, SIDE) + dx, SIDE)
            found.append(pltpu.make_async_remote_copy(
                staged.at[peer, m], out_ref.at[me, m], bs_sem.at[m], br_sem.at[m],
                device_id=(peer, sub), device_id_type=MESH))
        return found

    def own_copy(m):
        return pltpu.make_async_copy(staged.at[me, m], out_ref.at[me, m], own_sem.at[m])

    def member_body(m, _):
        pltpu.make_async_copy(ens_ref.at[m], ext.at[m, :, pl.ds(HALO, rows)], lsem.at[m]).wait()
        for cp in halo_copies(m):
            cp.wait()
        for t in range(tiles):
            hbuf[t, here] = ext[m, 0, :, cols_of(t)]

        def step_body(s, carry):
            for t, h_dy in spread(lambda t: hbuf[t, here], lane):
                u = ext[m, 1, :, cols_of(t)]
                v = ext[m, 2, :, cols_of(t)]
                u1 = u + ((DT * CORIOLIS) * v - half * (hbuf[t, above] - hbuf[t, below]))
                v1 = v - ((DT * CORIOLIS) * u + half * h_dy)
                d = dep[:, cols_of(t)]
                ext[m, 1, :, cols_of(t)] = u1
                ext[m, 2, :, cols_of(t)] = v1
                fbuf[t, here] = d * u1
                gbuf[t] = d * v1
            for t, g_dy in spread(lambda t: gbuf[t], lane):
                hbuf[t, here] = hbuf[t, here] - half * (fbuf[t, above] - fbuf[t, below] + g_dy)
            return carry

        lax.fori_loop(0, STEPS - 1, step_body, 0)
        inner = pl.ds(2 * HALO, rows)
        north, south = pl.ds(2 * HALO + 1, rows), pl.ds(2 * HALO - 1, rows)
        own = pl.ds(HALO, rows)
        for t, h_dy in spread(lambda t: hbuf[t, inner], lane[:rows]):
            u = ext[m, 1, :, cols_of(t)]
            v = ext[m, 2, :, cols_of(t)]
            u1 = u + ((DT * CORIOLIS) * v - half * (hbuf[t, above] - hbuf[t, below]))
            v1 = v[HALO:HALO + rows] - ((DT * CORIOLIS) * u[HALO:HALO + rows] + half * h_dy)
            d = dep[:, cols_of(t)]
            staged[t, m, 1] = u1[HALO:HALO + rows]
            staged[t, m, 2] = v1
            fbuf[t, here] = d * u1
            gbuf[t, own] = d[HALO:HALO + rows] * v1
        for t, g_dy in spread(lambda t: gbuf[t, own], lane[:rows]):
            staged[t, m, 0] = hbuf[t, inner] - half * (fbuf[t, north] - fbuf[t, south] + g_dy)
        own_copy(m).start()

        @pl.when(m < EARLY)
        def _():
            for cp in block_copies(m, 0, len(ORDER)):
                cp.start()

        @pl.when(m == EARLY)
        def _():
            for cp in block_copies(m, 0, SOME):
                cp.start()

        send_total(m)
        block = 256
        turned = jnp.concatenate(
            [jnp.transpose(jnp.concatenate([staged[t, m, 0] for t in range(4 * g, 4 * g + 4)], 0))
             for g in range(tiles // 4)], 1)
        parts = jnp.concatenate(split2(turned), 0)
        for q in range(nobs // block):
            span = slice(q * block, (q + 1) * block)
            hot = jnp.where(iota((tiles * rows, block), 0) == combo[:, span], 1.0, 0.0).astype(BF16)
            picked = nn(parts, hot)
            picked = picked[0:LANES] + picked[LANES:]
            got = jnp.sum(jnp.where(iota((LANES, block), 0) == lane_of[:, span], picked, 0.0), 0, keepdims=True)
            for s in range(block // LANES):
                mine[m + 1, pl.ds(q * (block // LANES) + s, 1), :] = got[:, s * LANES:(s + 1) * LANES]
        send_part(m + 1)
        return 0

    lax.fori_loop(0, members, member_body, 0)

    send_total(members)

    for cp in block_copies(EARLY, SOME, len(ORDER)):
        cp.start()

    def rest_body(m, _):
        for cp in block_copies(m, 0, len(ORDER)):
            cp.start()
        return 0

    lax.fori_loop(EARLY + 1, members, rest_body, 0)
    def totals_body(s, _):
        for sent, sems, count in ((part, s1_sem, n_sub), (prior_ref, s2_sem, n_mem), (prior_ref, r2_sem, n_mem)):
            peers = sent.at[pl.ds(0, count - 1), s]
            pltpu.make_async_copy(peers, peers, sems.at[s]).wait()
        return 0

    lax.fori_loop(0, members + 1, totals_body, 0)
    weights(prior_ref, obs_ref, val_ref, var_ref, at_ref, wt_ref, flat, heights, cuts,
            rows * n_sub, cols)

    def finish_body(m, _):
        peers = out_ref.at[pl.ds(0, n_mem - 1), m]
        for sems in (bs_sem, br_sem):
            pltpu.make_async_copy(peers, peers, sems.at[m]).wait()
        own_copy(m).wait()
        return 0

    lax.fori_loop(0, members, finish_body, 0)


def nn3(a, b):
    a_hi, a_lo = split2(a)
    b_hi, b_lo = split2(b)
    return nn(a_hi, b_hi) + (nn(a_hi, b_lo) + nn(a_lo, b_hi))


def weights(prior_ref, obs_ref, val_ref, var_ref, at_ref, wt_ref, flat, heights, cuts, size_x, size_y):
    n_mem, width, _, _ = prior_ref.shape
    batches, members, nobs = at_ref.shape
    groups = batches * nobs // LANES
    flat[...] = prior_ref[:, 1:].reshape(members * 8, LANES)
    cut = jnp.sum(prior_ref[:, 0], 0)
    cut = 1.0 / (cut * cut)
    for q in range(groups):
        b, s = q * LANES // nobs, q * LANES % nobs
        heights[b, :, s:s + LANES] = flat[pl.ds(q, members, stride=8), :]
        cuts[b, :, s:s + LANES] = cut[q:q + 1, :]
    scale = 1.0 / (members - 1)

    def batch_body(b, _):
        h = heights[b]
        mean = jnp.mean(h, 0, keepdims=True)
        at = h - mean
        inv_var = 1.0 / var_ref[pl.ds(b, 1), :]
        scaled = at * inv_var
        gram = nt(scaled, at, HIGHEST) * scale
        eye = jnp.where(iota((members, members), 0) == iota((members, members), 1), 1.0, 0.0)
        x = jnp.concatenate([eye, gram + eye], 1)
        line = iota(x.shape, 0)
        for k in range(0, members, 8):
            ahead = [jnp.broadcast_to(x[:, members + k + l:members + k + l + 1], x.shape) for l in range(8)]
            for j in range(0, 8, 2):
                p, q = k + j, k + j + 1
                col0, col1 = ahead[0], ahead[1]
                a, b01, c = col0[p:p + 1], col1[p:p + 1], col1[q:q + 1]
                inv = 1.0 / (a * c - b01 * b01)
                a, b01, c = a * inv, b01 * inv, c * inv

                def sweep(y):
                    row0 = c * y[p:p + 1] - b01 * y[q:q + 1]
                    row1 = a * y[q:q + 1] - b01 * y[p:p + 1]
                    left = y - col0 * row0 - col1 * row1
                    return jnp.where(line == p, row0, jnp.where(line == q, row1, left))

                ahead = [sweep(y) for y in ahead[2:]]
                x = sweep(x)
        inverse = x[:, 0:members]
        big = nn3(inverse, scaled)
        gap = (val_ref[pl.ds(b, 1), :] - mean) * inv_var
        lean = jnp.sum(at * gap, 1, keepdims=True)
        small = gap - scale * jnp.sum(big * lean, 0, keepdims=True)
        wt = small - 0.5 * big
        at_ref[b] = at * scale
        wt_ref[b] = wt

        here = obs_ref[pl.ds(b, 1), :]
        xy = jnp.concatenate(
            [jnp.broadcast_to(k.astype(F32), (4, nobs)) for k in (quot(here, size_y), rest(here, size_y))], 0)
        xy = jnp.transpose(xy)
        from_x = xy[:, 0:1]
        from_y = xy[:, 4:5]
        anom_hi, anom_lo = split2(jnp.transpose(at * scale))
        wt_hi, wt_lo = split2(wt)

        def carry_body(c, _):
            hc = heights[c]
            dev_hi, dev_lo = split2(hc - jnp.mean(hc, 0, keepdims=True))
            cross = nn(anom_hi, dev_hi) + (nn(anom_hi, dev_lo) + nn(anom_lo, dev_hi))
            there = obs_ref[pl.ds(c, 1), :]
            gx = jnp.abs(quot(there, size_y).astype(F32) - from_x)
            gx = jnp.minimum(gx, size_x - gx)
            gy = jnp.abs(rest(there, size_y).astype(F32) - from_y)
            gy = jnp.minimum(gy, size_y - gy)
            near = jnp.maximum(1.0 - (gx * gx + gy * gy) * cuts[c], 0.0)
            gain_hi, gain_lo = split2(cross * (near * near))
            heights[c] = hc + (nn(wt_hi, gain_hi) + (nn(wt_hi, gain_lo) + nn(wt_lo, gain_hi)))
            return 0

        lax.fori_loop(b + 1, batches, carry_body, 0)
        return 0

    lax.fori_loop(0, batches, batch_body, 0)


def forecast(ensemble, sea_depth, cutoff, obs, values, variance):
    per, fields, rows, cols = ensemble.shape
    n_mem = lax.axis_size("mem")
    n_sub = lax.axis_size("sub")
    members = per * n_mem
    batches, nobs = obs.shape
    total = batches * nobs
    tiles = cols // LANES
    slot = (per + 1, total // LANES, LANES)
    vmem = pl.BlockSpec(memory_space=pltpu.VMEM)
    hbm = pl.BlockSpec(memory_space=pl.ANY)
    dma = pltpu.SemaphoreType.DMA
    vm = pltpu.VMEM
    return pl.pallas_call(
        forecast_kernel,
        out_shape=(
            jax.ShapeDtypeStruct((n_mem, per, fields, rows, LANES), F32),
            jax.ShapeDtypeStruct((batches, members, nobs), F32),
            jax.ShapeDtypeStruct((batches, members, nobs), F32),
        ),
        in_specs=[hbm, hbm] + [vmem] * 4,
        out_specs=(hbm, vmem, vmem),
        scratch_shapes=[
            vm((per, fields, rows + 2 * HALO, cols), F32),
            vm((rows + 2 * HALO, cols), F32),
            vm((tiles, rows + 4 * HALO, LANES), F32),
            vm((tiles, rows + 4 * HALO, LANES), F32),
            vm((tiles, rows + 2 * HALO, LANES), F32),
            vm((n_sub, *slot), F32),
            vm(slot, F32),
            vm(slot, F32),
            vm((n_mem, *slot), F32),
            vm((tiles, per, fields, rows, LANES), F32),
            vm((members * 8, LANES), F32),
            vm((batches, members, nobs), F32),
            vm((batches, 1, nobs), F32),
            dma((per + 1,)), dma((2, per)), dma((2, per)), dma((2,)), dma((2,)),
            dma((per + 1,)), dma((per + 1,)), dma((per + 1,)), dma((per + 1,)),
            dma((per,)), dma((per,)), dma((per,)),
        ],
        compiler_params=pltpu.CompilerParams(
            collective_id=0, has_side_effects=True, vmem_limit_bytes=56 << 20),
        name="forecast",
    )(ensemble, sea_depth, cutoff, obs, values, variance)


def update_kernel(state_ref, at_hbm, wt_hbm, obs_ref, cut_ref, out_ref,
                  at_ref, wt_ref, lhs1, lhs2, far_x, sq_y, inv_r2, work, begin, stage, counts, in_sems, sems, w_sems):
    members, fields, rows, _ = state_ref.shape
    batches, _, nobs = at_ref.shape
    block = work.shape[2] // (fields * LANES)
    size_x = rows * lax.axis_size("sub")
    size_y = LANES * lax.axis_size("mem")
    x0 = lax.axis_index("sub") * rows
    y0 = lax.axis_index("mem") * LANES

    early = [pltpu.make_async_copy(at_hbm, at_ref, w_sems.at[0]), pltpu.make_async_copy(wt_hbm, wt_ref, w_sems.at[1])]
    for cp in early:
        cp.start()
    for step in range(rows // block):
        pltpu.make_async_copy(
            state_ref.at[:, :, pl.ds(step * block, block)], begin.at[step], in_sems.at[step]).start()
    cut = cut_ref[...].astype(F32)
    inv_r2[...] = 1.0 / (cut * cut)
    top = jnp.max(cut_ref[...])
    reach = top * top
    upper = jnp.where(iota((nobs, nobs), 0) < iota((nobs, nobs), 1), 1.0, 0.0).astype(BF16)

    def gap_to(pos, low, length, size):
        before = low - pos
        before = jnp.where(before < 0, before + size, before)
        after = pos - (low + length - 1)
        after = jnp.where(after < 0, after + size, after)
        inside = (pos >= low) & (pos < low + length)
        return jnp.where(inside, 0, jnp.minimum(before, after))

    def select(b, _):
        ox = quot(obs_ref[pl.ds(b, 1), :], size_y)
        oy = rest(obs_ref[pl.ds(b, 1), :], size_y)
        gx = gap_to(ox, x0, rows, size_x)
        gy = gap_to(oy, y0, LANES, size_y)
        keep = jnp.where(gx * gx + gy * gy < reach, 1.0, 0.0)
        rank = nn(jnp.broadcast_to(keep, (16, nobs)).astype(BF16), upper)[0:1]
        rank = jnp.where(keep > 0.5, rank, -1.0)
        total = jnp.sum(keep).astype(jnp.int32)
        chunks = (total + CHUNK - 1) // CHUNK
        counts[b] = chunks
        a = at_ref[b]
        a_hi, a_lo = split2(a - jnp.mean(a, 0, keepdims=True))
        w_hi, w_lo = split2(wt_ref[b])
        a3 = jnp.concatenate([a_hi, a_hi, a_lo], 0)
        w2 = jnp.concatenate([w_hi, w_lo], 1)

        def pack(c, _):
            want = (iota((CHUNK, nobs), 0) + c * CHUNK).astype(F32)
            hot = jnp.where(rank == want, 1.0, 0.0)
            hot16 = hot.astype(BF16)
            lhs1[b, c] = nt(hot16, a3).astype(BF16)
            zero = jnp.zeros_like(hot)
            turn = jnp.concatenate(
                [jnp.concatenate([hot, hot, zero], 0), jnp.concatenate([zero, zero, hot], 0)], 1).astype(BF16)
            lhs2[b, c] = nt(w2, turn).astype(BF16)
            px = jnp.sum(hot * ox.astype(F32), 1, keepdims=True)
            py = jnp.sum(hot * oy.astype(F32), 1, keepdims=True)
            far_x[b, c] = jnp.broadcast_to(px, (CHUNK, LANES))
            gy = jnp.abs((iota((CHUNK, LANES), 1) + y0).astype(F32) - py)
            gy = jnp.minimum(gy, size_y - gy)
            sq_y[b, c] = gy * gy
            return 0

        lax.fori_loop(0, chunks, pack, 0)
        return 0

    for cp in early:
        cp.wait()
    lax.fori_loop(0, batches, select, 0)

    slabs = fields * block
    steps = rows // block

    def place(s):
        return pl.ds(s % fields * block + s // fields, members, stride=slabs)

    def part(step):
        return pl.ds(pl.multiple_of(step * block, block), block)

    def in_copy(step):
        return pltpu.make_async_copy(state_ref.at[:, :, part(step)], begin.at[step], in_sems.at[step])

    def out_copy(step):
        return pltpu.make_async_copy(stage.at[step], out_ref.at[:, :, part(step)], sems.at[step])

    def step_body(step, _):
        in_copy(step).wait()
        source = begin.at[step].reshape(members * slabs, LANES)
        target = stage.at[step].reshape(members * slabs, LANES)
        for s in range(slabs):
            work[0, :, s * LANES:(s + 1) * LANES] = source[place(s), :]

        def batch_body(b, now):
            chunks = counts[b]

            def chunk_body(c, _):
                left = lhs1[b, c]
                right = lhs2[b, c]
                px = far_x[b, c]
                dy = sq_y[b, c]
                base = jnp.where(c == 0, now, 1 - now)
                for r in range(0, block, GROUP):
                    near = []
                    for k in range(r, r + GROUP):
                        row = step * block + k
                        gx = jnp.abs(px - (x0 + row).astype(F32))
                        gx = jnp.minimum(gx, size_x - gx)
                        ratio = (gx * gx + dy) * inv_r2[pl.ds(row, 1), :]
                        part = jnp.maximum(1.0 - ratio, 0.0)
                        near += [part * part] * fields
                    near = jnp.concatenate(near, 1)
                    span = slice(r * fields * LANES, (r + GROUP) * fields * LANES)
                    hi, lo = split2(work[now, :, span])
                    gain = nn(left, jnp.concatenate([hi, lo, hi], 0)) * near
                    top = gain.astype(BF16).astype(F32)
                    stacked = jnp.concatenate([top, gain - top, top], 0).astype(BF16)
                    work[1 - now, :, span] = work[base, :, span] + nn(right, stacked)
                return 0

            lax.fori_loop(0, chunks, chunk_body, 0)
            return jnp.where(chunks > 0, 1 - now, now)

        last = lax.fori_loop(0, batches, batch_body, 0)
        for s in range(slabs):
            target[place(s), :] = work[last, :, s * LANES:(s + 1) * LANES]
        out_copy(step).start()
        return 0

    lax.fori_loop(0, steps, step_body, 0)
    for step in range(steps):
        out_copy(step).wait()


def update(state, at, wt, obs, cutoff):
    members, fields, rows, _ = state.shape
    batches, _, nobs = at.shape
    block = 8
    chunks = pl.cdiv(nobs, CHUNK)
    vmem = pl.BlockSpec(memory_space=pltpu.VMEM)
    width = fields * block * LANES
    return pl.pallas_call(
        update_kernel,
        out_shape=jax.ShapeDtypeStruct(state.shape, F32),
        in_specs=[pl.BlockSpec(memory_space=pl.ANY)] * 3 + [vmem] * 2,
        out_specs=pl.BlockSpec(memory_space=pl.ANY),
        scratch_shapes=[
            pltpu.VMEM(at.shape, F32),
            pltpu.VMEM(wt.shape, F32),
            pltpu.VMEM((batches, chunks, CHUNK, 3 * members), BF16),
            pltpu.VMEM((batches, chunks, members, 3 * CHUNK), BF16),
            pltpu.VMEM((batches, chunks, CHUNK, LANES), F32),
            pltpu.VMEM((batches, chunks, CHUNK, LANES), F32),
            pltpu.VMEM((rows, LANES), F32),
            pltpu.VMEM((2, members, width), F32),
            pltpu.VMEM((rows // block, members, fields, block, LANES), F32),
            pltpu.VMEM((rows // block, members, fields, block, LANES), F32),
            pltpu.SMEM((batches,), jnp.int32),
            pltpu.SemaphoreType.DMA((rows // block,)),
            pltpu.SemaphoreType.DMA((rows // block,)),
            pltpu.SemaphoreType.DMA((2,)),
        ],
        compiler_params=pltpu.CompilerParams(vmem_limit_bytes=63 << 20),
        name="update",
    )(state, at, wt, obs, cutoff)


def local(ensemble, sea_depth, cutoff, obs_index, obs_value, obs_var):
    per, fields, rows, cols = ensemble.shape
    members = per * lax.axis_size("mem")
    state, at, wt = forecast(ensemble, sea_depth, cutoff, obs_index, obs_value, obs_var)
    return update(state.reshape(members, fields, rows, LANES), at, wt, obs_index, cutoff)


def solution(mesh):
    return jax.shard_map(
        local,
        mesh=mesh,
        in_specs=(P("mem", None, "sub", None), P("sub", None), P("sub", "mem"), P(), P(), P()),
        out_specs=P(None, None, "sub", "mem"),
        check_vma=False,
    )
```
